256 devices in a mesh: grp: 16 (over x, y), ln: 16 (over z, core).
Axes of the slice: x: 4, y: 4, z: 8, core: 2. Of those that a mesh axis runs over, the one named last changes fastest.
Arguments:
- object_field: float32 [2, 2, 2048, 2048], P(None, None, ('grp', 'ln')), may hold values from -6 to 6
- probe_wave: float32 [2, 128, 128], replicated, may hold values from -6 to 6
- measured: float32 [2, 1024, 128, 128], P(None, ('grp', 'ln')), may hold values from 0.1 to 3
- positions: int32 [2, 1024], P(None, 'grp'), may hold values from 0 to 2047
- shear_steps: int32 [2, 2048], P(None, ('grp', 'ln')), may hold values from -64 to 64
- smooth_weight: float32 [2048, 2048], P(('grp', 'ln')), may hold values from 0.05 to 0.24
Outputs:
- smoothed_step: float32 [2, 2, 2048, 2048], P(None, None, ('grp', 'ln'))
The draws below stay inside these ranges and needn't reach their ends.
Inputs may be any that keep to these rules, and one draw needn't show every extreme that they name: `positions`: a tile takes 128 columns from its first one on, wrapping around past the last column.
All inputs are finite; a program needn't handle non-finite values.
Results may differ from the reference program's by a relative error of at most 0.007.
Values may be sent and summed in bfloat16 or wider, within the bound.
No kernel may reach another device: no remote copies, remote signals or barrier semaphores. Data moves between devices by JAX's collectives and lax.ppermute only.
A program may use at most 64 MiB of HBM per device.

```python
import math
import jax
import jax.numpy as jnp
from jax import lax

COLS = 2048
TILE = 128
SLICES = 2
TILTS = 2
TILES_DEV = 4
ROWS = 2048
TILES = 1024
N_GRP = 16
N_LN = 16


def place_ends(result, stream_key, least, top_value):
    longest = result.shape.index(max(result.shape))
    spots = []
    for shift in (0, 1):
        where = [jax.random.randint(jax.random.fold_in(stream_key, axis), (), 0, length) for axis, length in enumerate(result.shape)]
        where[longest] = (where[longest] + shift) % result.shape[longest]
        spots.append(tuple(where))
    return result.at[spots[0]].set(least).at[spots[1]].set(top_value)


def block_scale(rng, shape, split, least, largest):
    def one(axis_at, blocks):
        heights = jax.random.uniform(jax.random.fold_in(jax.random.fold_in(rng, 6), axis_at), (blocks,), jnp.float32, least / len(split), largest / len(split))
        return jnp.repeat(jnp.exp(heights), shape[axis_at] // blocks).reshape((-1,) + (1,) * (len(shape) - axis_at - 1))

    level = one(*split[0])
    for cut in split[1:]:
        level = level * one(*cut)
    return level


def scatter_about(key, extent, width, limit, shards=(), kind=jnp.bfloat16):
    array = width * jax.random.normal(key, extent, jnp.float32)
    if shards:
        array = array * block_scale(key, extent, shards, -0.22, 0.18)
    return jnp.clip(array, -limit, limit).astype(kind)


def setup_inputs(seed: int = 0) -> dict:
    arg_keys = jax.random.split(jax.random.key(seed), 7)
    object_field = scatter_about(arg_keys[0], (SLICES, 2, ROWS, COLS), 1.0, 6.0, ((2, 256),), jnp.float32)
    probe_wave = scatter_about(arg_keys[1], (2, TILE, TILE), 1.0, 6.0, (), jnp.float32)
    measured = jnp.clip(jnp.exp(math.log(3.0) - 3.4011974 * jax.random.uniform(arg_keys[2], (TILTS, TILES, TILE, TILE), jnp.float32) ** block_scale(arg_keys[2], (TILTS, TILES, TILE, TILE), ((1, 256),), -0.2, 0.2)), 0.1, 3.0)
    positions = place_ends(jax.random.randint(arg_keys[3], (TILTS, TILES), 0, COLS), jax.random.fold_in(arg_keys[3], 1), 0, COLS - 1).astype(jnp.int32)
    shear_steps = place_ends(jax.random.randint(arg_keys[4], (TILTS, ROWS), -64, 65), jax.random.fold_in(arg_keys[4], 1), -64, 64).astype(jnp.int32)
    smooth_weight = jnp.clip(jnp.exp(math.log(0.24) - 1.5686159 * jax.random.uniform(arg_keys[5], (ROWS, COLS), jnp.float32) ** block_scale(arg_keys[5], (ROWS, COLS), ((0, 256),), -0.2, 0.2)), 0.05, 0.24)
    return dict(object_field=object_field, probe_wave=probe_wave, measured=measured, positions=positions, shear_steps=shear_steps, smooth_weight=smooth_weight)


AMP_FLOOR = 0.25
FRESNEL = 100.0
SHEAR_UNITS = 8

def signed_freq(length):
    counter = jnp.arange(length, dtype=jnp.int32)
    return (counter + length // 2) % length - length // 2

def reference(object_field, probe_wave, measured, positions, shear_steps, smooth_weight):
    columns = object_field.shape[-1]
    slices = object_field.shape[0]
    tilts = shear_steps.shape[0]
    tile = probe_wave.shape[-1]
    tiles_grp = TILES_DEV * N_LN
    obj_complex = object_field[:, 0] + 1j * object_field[:, 1]
    units = SHEAR_UNITS * columns
    turn_count = signed_freq(columns)[None, None, :] * shear_steps[:, :, None] % units
    angles = -2.0 * math.pi / units * turn_count.astype(jnp.float32)
    phase = jnp.cos(angles) + 1j * jnp.sin(angles)
    spectrum = jnp.fft.fft(obj_complex, axis=-1)
    sheared = jnp.fft.ifft(spectrum[None] * phase[:, None], axis=-1)
    sheared_re = lax.optimization_barrier(sheared.real.astype(jnp.bfloat16)).astype(jnp.float32)
    sheared_im = lax.optimization_barrier(sheared.imag.astype(jnp.bfloat16)).astype(jnp.float32)
    signed = signed_freq(tile)
    radius = signed[:, None, None] ** 2 + signed[None, None, :] ** 2
    kernel_angle = -FRESNEL / (tile * tile) * radius.astype(jnp.float32)
    kernel = jnp.cos(kernel_angle) + 1j * jnp.sin(kernel_angle)
    probe_complex = (probe_wave[0] + 1j * probe_wave[1])[:, None, :]
    offsets = jnp.arange(tile, dtype=jnp.int32)

    def transform(wave):
        return jnp.fft.fft2(wave, axes=(1, 3), norm='ortho')

    def inverse(wave):
        return jnp.fft.ifft2(wave, axes=(1, 3), norm='ortho')

    def one_band(group):
        row_start = (group * tile).astype(jnp.int32)
        band_re = lax.dynamic_slice_in_dim(sheared_re, row_start, tile, 2)
        band_im = lax.dynamic_slice_in_dim(sheared_im, row_start, tile, 2)
        band = band_re + 1j * band_im
        tile_start = (group * tiles_grp).astype(jnp.int32)
        starts = lax.dynamic_slice_in_dim(positions, tile_start, tiles_grp, 1)
        column_index = ((starts[:, :, None] + offsets) % columns).astype(jnp.int32)
        target = jnp.swapaxes(lax.dynamic_slice_in_dim(measured, tile_start, tiles_grp, 1), 1, 2)
        pieces = jnp.stack([band[tilt_num][:, :, column_index[tilt_num]] for tilt_num in range(tilts)])
        wave = probe_complex
        incoming = []
        exit_wave = wave
        for layer in range(slices):
            incoming.append(wave)
            exit_wave = wave * pieces[:, layer]
            if layer + 1 < slices:
                wave = inverse(transform(exit_wave) * kernel)
        far = transform(exit_wave)
        amplitude = jnp.sqrt(far.real * far.real + far.imag * far.imag + AMP_FLOOR)
        back = inverse((1.0 - target / amplitude) * far)
        gradients = [None] * slices
        for layer in reversed(range(slices)):
            gradients[layer] = jnp.conj(incoming[layer]) * back
            if layer > 0:
                back = inverse(transform(jnp.conj(pieces[:, layer]) * back) * jnp.conj(kernel))
        grads = jnp.stack(gradients, axis=1)
        grad_re = lax.optimization_barrier(grads.real.astype(jnp.bfloat16)).astype(jnp.float32)
        grad_im = lax.optimization_barrier(grads.imag.astype(jnp.bfloat16)).astype(jnp.float32)
        rounded = grad_re + 1j * grad_im
        summed = jnp.stack([jnp.zeros((slices, tile, columns), rounded.dtype).at[:, :, column_index[tilt_num]].add(rounded[tilt_num]) for tilt_num in range(tilts)])
        return summed
    bands = lax.map(one_band, jnp.arange(N_GRP, dtype=jnp.int32))
    bands = jnp.transpose(bands, (1, 2, 0, 3, 4)).reshape(tilts, slices, N_GRP * tile, columns)
    descent = lax.optimization_barrier(jnp.sum(jnp.fft.ifft(jnp.fft.fft(bands, axis=-1) * jnp.conj(phase)[:, None], axis=-1), axis=0))
    padded = jnp.pad(descent, ((0, 0), (1, 1), (0, 0)))
    neighbours = padded[:, :-2] + padded[:, 2:] + jnp.roll(descent, 1, axis=2) + jnp.roll(descent, -1, axis=2)
    smoothed = descent + smooth_weight * (neighbours - 4.0 * descent)
    return jnp.stack((smoothed.real, smoothed.imag), axis=1)
```

```python
import functools
import math

import jax
import jax.numpy as jnp
import numpy as np
from jax import lax
from jax.experimental import pallas as pl
from jax.experimental.pallas import tpu as pltpu
from jax.sharding import PartitionSpec as P

AMP_FLOOR = 0.25
FRESNEL = 100.0
SHEAR_UNITS = 8
LANES = 128
OUTER = 16
COLS = OUTER * LANES
ROWS = 8
BF16 = jnp.bfloat16
F32 = jnp.float32


def split_table(table):
    high = np.asarray(table, np.float32).astype(BF16)
    low = (np.asarray(table) - high.astype(np.float64)).astype(np.float32).astype(BF16)
    return np.stack([high, low])


def right_block(matrix):
    top = np.concatenate([matrix.real, matrix.imag], 1)
    bottom = np.concatenate([-matrix.imag, matrix.real], 1)
    return np.concatenate([top, bottom], 0)


def tables():
    counter = np.arange(LANES)
    signed = (counter + LANES // 2) % LANES - LANES // 2
    dft = np.exp(-2j * math.pi / LANES * (counter[:, None] * counter[None, :] % LANES))
    dft = dft / math.sqrt(LANES)
    step = np.exp(-1j * FRESNEL / LANES**2 * signed.astype(np.float64) ** 2)
    spread = (dft.conj() * step[None, :]) @ dft
    fourier = right_block(dft)
    fresnel = right_block(spread)
    return np.stack([split_table(t) for t in (fourier, fourier.T, fresnel, fresnel.T)])


def twiddles():
    turn = np.arange(OUTER)[:, None] * np.arange(LANES)[None, :]
    angle = 2.0 * math.pi / COLS * turn
    return np.stack([np.cos(angle), np.sin(angle)]).astype(np.float32)


def const_mul(value, angle_num, angle_den, sign):
    re, im = value
    eighth = 8 * angle_num / angle_den
    if eighth == 0:
        return value
    if eighth == 2:
        return (-im * sign, re * sign) if sign in (1, -1) else None
    cosine = math.cos(2.0 * math.pi * angle_num / angle_den)
    sine = sign * math.sin(2.0 * math.pi * angle_num / angle_den)
    return (re * cosine - im * sine, re * sine + im * cosine)


def small_dft(values, sign):
    count = len(values)
    if count == 1:
        return values
    even = small_dft(values[::2], sign)
    odd = small_dft(values[1::2], sign)
    out = [None] * count
    for k in range(count // 2):
        re, im = const_mul(odd[k], k, count, sign)
        out[k] = (even[k][0] + re, even[k][1] + im)
        out[k + count // 2] = (even[k][0] - re, even[k][1] - im)
    return out


def cmul(a, b):
    return (a[0] * b[0] - a[1] * b[1], a[0] * b[1] + a[1] * b[0])


def conj_mul(a, b):
    return (a[0] * b[0] + a[1] * b[1], a[0] * b[1] - a[1] * b[0])


def halves(x):
    high = x.astype(BF16)
    return high, (x - high.astype(F32)).astype(BF16)


def dot(a, b):
    return jnp.dot(a, b, preferred_element_type=F32)


def rmul(x, table, which):
    high, low = halves(x)
    top = table[which, 0]
    return dot(high, top) + (dot(low, top) + dot(high, table[which, 1]))


def lmul(table, which, x):
    high, low = halves(x)
    top = table[which, 0]
    return dot(top, high) + (dot(top, low) + dot(table[which, 1], high))


def shear_factors(shear, tilt):
    row = lax.broadcasted_iota(jnp.int32, (ROWS, LANES), 0)
    lane = lax.broadcasted_iota(jnp.int32, (ROWS, LANES), 1)
    steps = jnp.zeros((ROWS, LANES), jnp.int32)
    for r in range(ROWS):
        steps = jnp.where(row == r, shear[tilt, r], steps)
    units = SHEAR_UNITS * COLS

    def turn(count):
        count = jnp.bitwise_and(count, units - 1)
        count = jnp.where(count >= units // 2, count - units, count)
        angle = (-2.0 * math.pi / units) * count.astype(F32)
        return (jnp.cos(angle), jnp.sin(angle))

    freq = OUTER * lane - jnp.where(lane >= LANES // 2, COLS, 0)
    base = turn(freq * steps)
    first = turn(steps)
    powers = [(jnp.ones((ROWS, LANES), F32), jnp.zeros((ROWS, LANES), F32)), first]
    for i in range(2, OUTER):
        powers.append(cmul(powers[i // 2], powers[i - i // 2]))
    return base, powers


def put(ref, block, value):
    ref[block * ROWS : (block + 1) * ROWS, :LANES] = value[0]
    ref[block * ROWS : (block + 1) * ROWS, LANES:] = value[1]


def get(array, block):
    return (
        array[block * ROWS : (block + 1) * ROWS, :LANES],
        array[block * ROWS : (block + 1) * ROWS, LANES:],
    )


def forward_columns(chunks, tw, ref, base_block):
    mixed = small_dft(chunks, -1)
    for i in range(OUTER):
        w = (tw[0, i : i + 1, :], tw[1, i : i + 1, :])
        put(ref, base_block + i, conj_mul(w, mixed[i]))


def inverse_columns(array, base_block, tw):
    blocks = []
    for i in range(OUTER):
        w = (tw[0, i : i + 1, :] * (1.0 / OUTER), tw[1, i : i + 1, :] * (1.0 / OUTER))
        blocks.append(cmul(w, get(array, base_block + i)))
    return small_dft(blocks, 1)


def shear_kernel(shear, pos, obj, table, tw, out, x_ref, y_ref, z_ref, band):
    slices = obj.shape[0]
    tilts = band.shape[0]
    for s in range(slices):
        chunks = [
            tuple(obj[s, c, :, j * LANES : (j + 1) * LANES] for c in range(2)) for j in range(OUTER)
        ]
        forward_columns(chunks, tw, x_ref, s * OUTER)
    x_ref[...] = rmul(x_ref[...], table, 0)
    for t in range(tilts):
        base, powers = shear_factors(shear, t)
        for i in range(OUTER):
            phase = cmul(base, powers[i])
            for s in range(slices):
                put(y_ref, (t * slices + s) * OUTER + i, cmul(get(x_ref, s * OUTER + i), phase))
    z_ref[...] = rmul(y_ref[...], table, 1)
    for t in range(tilts):
        for s in range(slices):
            chunks = inverse_columns(z_ref, (t * slices + s) * OUTER, tw)
            for j in range(OUTER):
                for c in range(2):
                    row = (2 * s + c) * ROWS
                    band[t, row : row + ROWS, j * LANES : (j + 1) * LANES] = chunks[j][c]
                    if j == 0:
                        band[t, row : row + ROWS, COLS:] = chunks[j][c]
    depth = band.shape[1]
    lane = lax.broadcasted_iota(jnp.int32, (depth, LANES), 1)
    per_owner = out.shape[1] // tilts

    def owner(d, carry):
        for jj in range(per_owner):
            for t in range(tilts):
                p = pos[t, d * per_owner + jj]
                start = pl.multiple_of((p // LANES) * LANES, LANES)
                off = p % LANES
                back = (LANES - off) % LANES
                near = pltpu.roll(band[t, :, pl.ds(start, LANES)], back, 1)
                far = pltpu.roll(band[t, :, pl.ds(start + LANES, LANES)], back, 1)
                out[d, t * per_owner + jj] = jnp.where(lane < LANES - off, near, far).astype(BF16)
        return carry

    lax.fori_loop(0, out.shape[0], owner, 0)


def both(value, table, right, left):
    re, im = value
    tile = LANES
    half = rmul(jnp.concatenate([re, im], 1), table, right)
    stacked = jnp.concatenate(
        [
            jnp.concatenate([half[:tile, :tile], half[tile:, :tile]], 1),
            jnp.concatenate([half[:tile, tile:], half[tile:, tile:]], 1),
        ],
        0,
    )
    full = lmul(table, left, stacked)
    return (
        jnp.concatenate([full[:tile, :tile], full[:tile, tile:]], 0),
        jnp.concatenate([full[tile:, :tile], full[tile:, tile:]], 0),
    )


def tile_kernel(recv, measured, probe, table, out):
    owners = recv.shape[0]
    pair = recv.shape[1]
    parts = [[] for _ in range(4)]
    for p in range(pair):
        for d in range(owners):
            rows = recv[d, p].astype(F32)
            for k in range(4):
                parts[k].append(rows[k * ROWS : (k + 1) * ROWS])
    parts = [jnp.concatenate(part, 0) for part in parts]
    first, second = (parts[0], parts[1]), (parts[2], parts[3])
    start = tuple(jnp.concatenate([probe[c]] * pair, 0) for c in range(2))
    target = jnp.concatenate([measured[p] for p in range(pair)], 0)
    wave = both(cmul(start, first), table, 2, 3)
    far = both(cmul(wave, second), table, 0, 1)
    factor = 1.0 - target * lax.rsqrt(far[0] * far[0] + far[1] * far[1] + AMP_FLOOR)
    back = both((factor * far[0], factor * far[1]), table, 1, 0)
    grad1 = conj_mul(wave, back)
    back = both(conj_mul(second, back), table, 3, 2)
    grad0 = conj_mul(start, back)
    for p in range(pair):
        for d in range(owners):
            row = p * LANES + d * ROWS
            out[d, p] = jnp.concatenate(
                [g[row : row + ROWS] for g in (*grad0, *grad1)], 0
            ).astype(BF16)


def descent_kernel(shear, pos, recv, weight, table, tw, out, edges, acc, x_ref, y_ref):
    tilts = acc.shape[0]
    per_owner = recv.shape[1] // tilts
    depth = acc.shape[1]
    slices = depth // (2 * ROWS)
    acc[...] = jnp.zeros_like(acc)
    lane = lax.broadcasted_iota(jnp.int32, (depth, LANES), 1)

    def owner(d, carry):
        for jj in range(per_owner):
            for t in range(tilts):
                p = pos[t, d * per_owner + jj]
                start = pl.multiple_of((p // LANES) * LANES, LANES)
                off = p % LANES
                moved = pltpu.roll(recv[d, t * per_owner + jj].astype(F32), off, 1)
                here = lane >= off
                acc[t, :, pl.ds(start, LANES)] += jnp.where(here, moved, 0.0)
                acc[t, :, pl.ds(start + LANES, LANES)] += jnp.where(here, 0.0, moved)
        return carry

    lax.fori_loop(0, recv.shape[0], owner, 0)
    for t in range(tilts):
        for s in range(slices):
            chunks = []
            for j in range(OUTER):
                pair = []
                for c in range(2):
                    row = (2 * s + c) * ROWS
                    value = acc[t, row : row + ROWS, j * LANES : (j + 1) * LANES]
                    if j == 0:
                        value = value + acc[t, row : row + ROWS, COLS:]
                    pair.append(value)
                chunks.append(tuple(pair))
            forward_columns(chunks, tw, x_ref, (t * slices + s) * OUTER)
    x_ref[...] = rmul(x_ref[...], table, 0)
    for t in range(tilts):
        base, powers = shear_factors(shear, t)
        for i in range(OUTER):
            phase = cmul(base, powers[i])
            for s in range(slices):
                value = conj_mul(phase, get(x_ref, (t * slices + s) * OUTER + i))
                if t:
                    before = get(y_ref, s * OUTER + i)
                    value = (value[0] + before[0], value[1] + before[1])
                put(y_ref, s * OUTER + i, value)
    y_ref[...] = rmul(y_ref[...], table, 1)
    row = lax.broadcasted_iota(jnp.int32, (ROWS, LANES), 0)
    lane = lax.broadcasted_iota(jnp.int32, (ROWS, LANES), 1)
    for s in range(slices):
        chunks = inverse_columns(y_ref, s * OUTER, tw)
        for c in range(2):
            values = [chunk[c] for chunk in chunks]
            ahead = [pltpu.roll(v, 1, 1) for v in values]
            behind = [pltpu.roll(v, LANES - 1, 1) for v in values]
            for j in range(OUTER):
                v = values[j]
                cols = slice(j * LANES, (j + 1) * LANES)
                left = jnp.where(lane == 0, ahead[j - 1], ahead[j])
                right = jnp.where(lane == LANES - 1, behind[(j + 1) % OUTER], behind[j])
                above = jnp.where(row == 0, 0.0, pltpu.roll(v, 1, 0))
                below = jnp.where(row == ROWS - 1, 0.0, pltpu.roll(v, ROWS - 1, 0))
                around = (above + below) + (left + right)
                out[s, c, :, cols] = v + weight[:, cols] * (around - 4.0 * v)
                edges[0, 2 * s + c : 2 * s + c + 1, cols] = v[:1]
                edges[1, 2 * s + c : 2 * s + c + 1, cols] = v[ROWS - 1 :]


VMEM = pl.BlockSpec(memory_space=pltpu.VMEM)
SMEM = pl.BlockSpec(memory_space=pltpu.SMEM)


def per_device(object_field, probe_wave, measured, positions, shear_steps, smooth_weight):
    slices = object_field.shape[0]
    tilts, per_owner = measured.shape[:2]
    owners = lax.axis_size("ln")
    tiles = tilts * per_owner
    depth = 2 * slices * ROWS
    table = jnp.asarray(tables())
    tw = jnp.asarray(twiddles())
    rows = slices * OUTER * ROWS
    chunk = (owners, tiles, depth, LANES)
    send = pl.pallas_call(
        shear_kernel,
        out_shape=jax.ShapeDtypeStruct(chunk, BF16),
        in_specs=[SMEM, SMEM, VMEM, VMEM, VMEM],
        out_specs=VMEM,
        scratch_shapes=[
            pltpu.VMEM((rows, 2 * LANES), F32),
            pltpu.VMEM((tilts * rows, 2 * LANES), F32),
            pltpu.VMEM((tilts * rows, 2 * LANES), F32),
            pltpu.VMEM((tilts, depth, COLS + LANES), F32),
        ],
        name="shear",
    )(shear_steps, positions, object_field, table[:2], tw)
    recv = lax.all_to_all(send, "ln", 0, 0, tiled=True)
    pair = 2
    grads = pl.pallas_call(
        tile_kernel,
        out_shape=jax.ShapeDtypeStruct(chunk, BF16),
        grid=(tiles // pair,),
        in_specs=[
            pl.BlockSpec((owners, pair, depth, LANES), lambda g: (0, g, 0, 0)),
            pl.BlockSpec((pair, LANES, LANES), lambda g: (g, 0, 0)),
            pl.BlockSpec((2, LANES, LANES), lambda g: (0, 0, 0)),
            pl.BlockSpec(table.shape, lambda g: (0, 0, 0, 0)),
        ],
        out_specs=pl.BlockSpec((owners, pair, depth, LANES), lambda g: (0, g, 0, 0)),
        name="tiles",
    )(recv, measured.reshape(tiles, LANES, LANES), probe_wave, table)
    back = lax.all_to_all(grads, "ln", 0, 0, tiled=True)
    partial, edges = pl.pallas_call(
        descent_kernel,
        out_shape=(
            jax.ShapeDtypeStruct((slices, 2, ROWS, COLS), F32),
            jax.ShapeDtypeStruct((2, 2 * slices, COLS), F32),
        ),
        in_specs=[SMEM, SMEM, VMEM, VMEM, VMEM, VMEM],
        out_specs=(VMEM, VMEM),
        scratch_shapes=[
            pltpu.VMEM((tilts, depth, COLS + LANES), F32),
            pltpu.VMEM((tilts * rows, 2 * LANES), F32),
            pltpu.VMEM((rows, 2 * LANES), F32),
        ],
        name="descent",
    )(shear_steps, positions, back, smooth_weight, table[:2], tw)
    count = lax.axis_size("grp") * owners
    above = lax.ppermute(edges[1], ("grp", "ln"), [(i, i + 1) for i in range(count - 1)])
    below = lax.ppermute(edges[0], ("grp", "ln"), [(i + 1, i) for i in range(count - 1)])
    shape = (slices, 2, 1, COLS)
    gap = jnp.zeros((slices, 2, ROWS - 2, COLS), F32)
    outside = jnp.concatenate([above.reshape(shape), gap, below.reshape(shape)], 2)
    return partial + smooth_weight * outside


def solution(mesh):
    in_specs = (
        P(None, None, ("grp", "ln"), None),
        P(),
        P(None, ("grp", "ln"), None, None),
        P(None, "grp"),
        P(None, ("grp", "ln")),
        P(("grp", "ln"), None),
    )
    out_specs = P(None, None, ("grp", "ln"), None)
    return jax.shard_map(
        per_device, mesh=mesh, in_specs=in_specs, out_specs=out_specs, check_vma=False
    )
```

```python
import functools
import math

import jax
import jax.numpy as jnp
import numpy as np
from jax import lax
from jax.experimental import pallas as pl
from jax.experimental.pallas import tpu as pltpu
from jax.sharding import PartitionSpec as P

AMP_FLOOR = 0.25
FRESNEL = 100.0
SHEAR_UNITS = 8
LANES = 128
OUTER = 16
COLS = OUTER * LANES
ROWS = 8
UNROLL = 4
BF16 = jnp.bfloat16
F32 = jnp.float32


def split_table(table):
    high = np.asarray(table, np.float32).astype(BF16)
    low = (np.asarray(table) - high.astype(np.float64)).astype(np.float32).astype(BF16)
    return np.stack([high, low])


def right_block(matrix):
    top = np.concatenate([matrix.real, matrix.imag], 1)
    bottom = np.concatenate([-matrix.imag, matrix.real], 1)
    return np.concatenate([top, bottom], 0)


def tables():
    counter = np.arange(LANES)
    signed = (counter + LANES // 2) % LANES - LANES // 2
    dft = np.exp(-2j * math.pi / LANES * (counter[:, None] * counter[None, :] % LANES))
    dft = dft / math.sqrt(LANES)
    step = np.exp(-1j * FRESNEL / LANES**2 * signed.astype(np.float64) ** 2)
    spread = (dft.conj() * step[None, :]) @ dft
    fourier = right_block(dft)
    fresnel = right_block(spread)
    return np.stack([split_table(t) for t in (fourier, fourier.T, fresnel, fresnel.T)])


def twiddles():
    turn = np.arange(OUTER)[:, None] * np.arange(LANES)[None, :]
    angle = 2.0 * math.pi / COLS * turn
    return np.stack([np.cos(angle), np.sin(angle)]).astype(np.float32)


def const_mul(value, angle_num, angle_den, sign):
    re, im = value
    eighth = 8 * angle_num / angle_den
    if eighth == 0:
        return value
    if eighth == 2:
        return (-im * sign, re * sign) if sign in (1, -1) else None
    cosine = math.cos(2.0 * math.pi * angle_num / angle_den)
    sine = sign * math.sin(2.0 * math.pi * angle_num / angle_den)
    return (re * cosine - im * sine, re * sine + im * cosine)


def small_dft(values, sign):
    count = len(values)
    if count == 1:
        return values
    even = small_dft(values[::2], sign)
    odd = small_dft(values[1::2], sign)
    out = [None] * count
    for k in range(count // 2):
        re, im = const_mul(odd[k], k, count, sign)
        out[k] = (even[k][0] + re, even[k][1] + im)
        out[k + count // 2] = (even[k][0] - re, even[k][1] - im)
    return out


def cmul(a, b):
    return (a[0] * b[0] - a[1] * b[1], a[0] * b[1] + a[1] * b[0])


def conj_mul(a, b):
    return (a[0] * b[0] + a[1] * b[1], a[0] * b[1] - a[1] * b[0])


def halves(x):
    high = x.astype(BF16)
    return high, (x - high.astype(F32)).astype(BF16)


def dot(a, b):
    return jnp.dot(a, b, preferred_element_type=F32)


def rmul(x, table, which):
    high, low = halves(x)
    top = table[which, 0]
    return dot(high, top) + (dot(low, top) + dot(high, table[which, 1]))


def lmul(table, which, x):
    high, low = halves(x)
    top = table[which, 0]
    return dot(top, high) + (dot(top, low) + dot(table[which, 1], high))


def shear_factors(shear, tilt):
    row = lax.broadcasted_iota(jnp.int32, (ROWS, LANES), 0)
    lane = lax.broadcasted_iota(jnp.int32, (ROWS, LANES), 1)
    steps = jnp.zeros((ROWS, LANES), jnp.int32)
    for r in range(ROWS):
        steps = jnp.where(row == r, shear[tilt, r], steps)
    units = SHEAR_UNITS * COLS

    def turn(count):
        count = jnp.bitwise_and(count, units - 1)
        count = jnp.where(count >= units // 2, count - units, count)
        angle = (-2.0 * math.pi / units) * count.astype(F32)
        return (jnp.cos(angle), jnp.sin(angle))

    freq = OUTER * lane - jnp.where(lane >= LANES // 2, COLS, 0)
    base = turn(freq * steps)
    first = turn(steps)
    powers = [(jnp.ones((ROWS, LANES), F32), jnp.zeros((ROWS, LANES), F32)), first]
    for i in range(2, OUTER):
        powers.append(cmul(powers[i // 2], powers[i - i // 2]))
    return base, powers


def put(ref, block, value):
    ref[block * ROWS : (block + 1) * ROWS, :LANES] = value[0]
    ref[block * ROWS : (block + 1) * ROWS, LANES:] = value[1]


def get(array, block):
    return (
        array[block * ROWS : (block + 1) * ROWS, :LANES],
        array[block * ROWS : (block + 1) * ROWS, LANES:],
    )


def forward_columns(chunks, tw, ref, base_block):
    mixed = small_dft(chunks, -1)
    for i in range(OUTER):
        w = (tw[0, i : i + 1, :], tw[1, i : i + 1, :])
        put(ref, base_block + i, conj_mul(w, mixed[i]))


def inverse_columns(array, base_block, tw):
    blocks = []
    for i in range(OUTER):
        w = (tw[0, i : i + 1, :] * (1.0 / OUTER), tw[1, i : i + 1, :] * (1.0 / OUTER))
        blocks.append(cmul(w, get(array, base_block + i)))
    return small_dft(blocks, 1)


def shear_kernel(shear, pos, obj, table, tw, out, x_ref, y_ref, z_ref, band):
    slices = obj.shape[0]
    tilts = band.shape[0]
    for s in range(slices):
        chunks = [
            tuple(obj[s, c, :, j * LANES : (j + 1) * LANES] for c in range(2)) for j in range(OUTER)
        ]
        forward_columns(chunks, tw, x_ref, s * OUTER)
    x_ref[...] = rmul(x_ref[...], table, 0)
    for t in range(tilts):
        base, powers = shear_factors(shear, t)
        for i in range(OUTER):
            phase = cmul(base, powers[i])
            for s in range(slices):
                put(y_ref, (t * slices + s) * OUTER + i, cmul(get(x_ref, s * OUTER + i), phase))
    z_ref[...] = rmul(y_ref[...], table, 1)
    for t in range(tilts):
        for s in range(slices):
            chunks = inverse_columns(z_ref, (t * slices + s) * OUTER, tw)
            for j in range(OUTER):
                for c in range(2):
                    row = (2 * s + c) * ROWS
                    band[t, row : row + ROWS, j * LANES : (j + 1) * LANES] = chunks[j][c]
                    if j == 0:
                        band[t, row : row + ROWS, COLS:] = chunks[j][c]
    depth = band.shape[1]
    lane = lax.broadcasted_iota(jnp.int32, (depth, LANES), 1)
    per_owner = out.shape[1] // tilts

    def some_owners(step, carry):
        for o in range(UNROLL):
            d = step * UNROLL + o
            for jj in range(per_owner):
                for t in range(tilts):
                    p = pos[t, d * per_owner + jj]
                    off = jnp.bitwise_and(p, LANES - 1)
                    start = pl.multiple_of(p - off, LANES)
                    back = jnp.bitwise_and(LANES - off, LANES - 1)
                    near = pltpu.roll(band[t, :, pl.ds(start, LANES)], back, 1)
                    far = pltpu.roll(band[t, :, pl.ds(start + LANES, LANES)], back, 1)
                    window = jnp.where(lane < LANES - off, near, far)
                    out[d, t * per_owner + jj] = window.astype(BF16)
        return carry

    lax.fori_loop(0, out.shape[0] // UNROLL, some_owners, 0)


def both(values, table, right, left):
    tile = LANES
    halved = [rmul(jnp.concatenate(value, 1), table, right) for value in values]
    stacked = [
        jnp.concatenate(
            [
                jnp.concatenate([half[:tile, :tile], half[tile:, :tile]], 1),
                jnp.concatenate([half[:tile, tile:], half[tile:, tile:]], 1),
            ],
            0,
        )
        for half in halved
    ]
    full = [lmul(table, left, x) for x in stacked]
    return [
        (
            jnp.concatenate([x[:tile, :tile], x[:tile, tile:]], 0),
            jnp.concatenate([x[tile:, :tile], x[tile:, tile:]], 0),
        )
        for x in full
    ]


def tile_kernel(recv, measured, probe, table, out):
    owners = recv.shape[0]
    pairs = recv.shape[1] // 2
    first, second, target = [], [], []
    for q in range(pairs):
        parts = [[] for _ in range(4)]
        for p in (2 * q, 2 * q + 1):
            for d in range(owners):
                rows = recv[d, p].astype(F32)
                for k in range(4):
                    parts[k].append(rows[k * ROWS : (k + 1) * ROWS])
        parts = [jnp.concatenate(part, 0) for part in parts]
        first.append((parts[0], parts[1]))
        second.append((parts[2], parts[3]))
        target.append(jnp.concatenate([measured[2 * q], measured[2 * q + 1]], 0))
    start = tuple(jnp.concatenate([probe[c]] * 2, 0) for c in range(2))
    wave = both([cmul(start, x) for x in first], table, 2, 3)
    far = both([cmul(w, x) for w, x in zip(wave, second)], table, 0, 1)
    changed = []
    for (re, im), m in zip(far, target):
        factor = 1.0 - m * lax.rsqrt(re * re + im * im + AMP_FLOOR)
        changed.append((factor * re, factor * im))
    back = both(changed, table, 1, 0)
    grad1 = [conj_mul(w, b) for w, b in zip(wave, back)]
    back = both([conj_mul(x, b) for x, b in zip(second, back)], table, 3, 2)
    grad0 = [conj_mul(start, b) for b in back]
    for q in range(pairs):
        grads = (*grad0[q], *grad1[q])
        for p in range(2):
            for d in range(owners):
                row = p * LANES + d * ROWS
                mine = jnp.concatenate([g[row : row + ROWS] for g in grads], 0)
                out[d, 2 * q + p] = mine.astype(BF16)


def descent_kernel(shear, pos, recv, weight, table, tw, out, near, far, *scratch):
    accs, (x_ref, y_ref) = scratch[:-2], scratch[-2:]
    tilts = len(accs) // 2
    per_owner = recv.shape[1] // tilts
    depth = accs[0].shape[0]
    slices = depth // (2 * ROWS)
    for acc in accs:
        acc[...] = jnp.zeros_like(acc)
    lane = lax.broadcasted_iota(jnp.int32, (depth, LANES), 1)

    def some_owners(step, carry):
        for o in range(UNROLL):
            d = step * UNROLL + o
            for jj in range(per_owner):
                for t in range(tilts):
                    acc = accs[t + tilts * (jj % 2)]
                    p = pos[t, d * per_owner + jj]
                    off = jnp.bitwise_and(p, LANES - 1)
                    start = pl.multiple_of(p - off, LANES)
                    moved = pltpu.roll(recv[d, t * per_owner + jj].astype(F32), off, 1)
                    here = lane >= off
                    spread = [jnp.where(here, moved, 0.0), jnp.where(here, 0.0, moved)]
                    acc[:, pl.ds(start, 2 * LANES)] += jnp.concatenate(spread, 1)
        return carry

    lax.fori_loop(0, recv.shape[0] // UNROLL, some_owners, 0)
    for t in range(tilts):
        for s in range(slices):
            chunks = []
            for j in range(OUTER):
                pair = []
                for c in range(2):
                    row = (2 * s + c) * ROWS
                    value = 0.0
                    for acc in (accs[t], accs[t + tilts]):
                        value = value + acc[row : row + ROWS, j * LANES : (j + 1) * LANES]
                        if j == 0:
                            value = value + acc[row : row + ROWS, COLS:]
                    pair.append(value)
                chunks.append(tuple(pair))
            forward_columns(chunks, tw, x_ref, (t * slices + s) * OUTER)
    x_ref[...] = rmul(x_ref[...], table, 0)
    for t in range(tilts):
        base, powers = shear_factors(shear, t)
        for i in range(OUTER):
            phase = cmul(base, powers[i])
            for s in range(slices):
                value = conj_mul(phase, get(x_ref, (t * slices + s) * OUTER + i))
                if t:
                    before = get(y_ref, s * OUTER + i)
                    value = (value[0] + before[0], value[1] + before[1])
                put(y_ref, s * OUTER + i, value)
    y_ref[...] = rmul(y_ref[...], table, 1)
    row = lax.broadcasted_iota(jnp.int32, (ROWS, LANES), 0)
    lane = lax.broadcasted_iota(jnp.int32, (ROWS, LANES), 1)
    odd = lax.rem(lax.axis_index("ln"), 2) == 1
    for s in range(slices):
        chunks = inverse_columns(y_ref, s * OUTER, tw)
        for c in range(2):
            values = [chunk[c] for chunk in chunks]
            ahead = [pltpu.roll(v, 1, 1) for v in values]
            behind = [pltpu.roll(v, LANES - 1, 1) for v in values]
            for j in range(OUTER):
                v = values[j]
                cols = slice(j * LANES, (j + 1) * LANES)
                left = jnp.where(lane == 0, ahead[j - 1], ahead[j])
                right = jnp.where(lane == LANES - 1, behind[(j + 1) % OUTER], behind[j])
                above = jnp.where(row == 0, 0.0, pltpu.roll(v, 1, 0))
                below = jnp.where(row == ROWS - 1, 0.0, pltpu.roll(v, ROWS - 1, 0))
                around = (above + below) + (left + right)
                out[s, c, :, cols] = v + weight[:, cols] * (around - 4.0 * v)
                first, last = v[:1], v[ROWS - 1 :]
                near[2 * s + c : 2 * s + c + 1, cols] = jnp.where(odd, first, last)
                far[2 * s + c : 2 * s + c + 1, cols] = jnp.where(odd, last, first)


def halo_kernel(partial, near, far, weight, out):
    odd = lax.rem(lax.axis_index("ln"), 2) == 1
    row = lax.broadcasted_iota(jnp.int32, weight.shape, 0)
    near_row = jnp.where(odd, 0, ROWS - 1)
    at_near = jnp.where(row == near_row, weight[...], 0.0)
    at_far = jnp.where(row == ROWS - 1 - near_row, weight[...], 0.0)
    for s in range(out.shape[0]):
        for c in range(2):
            k = 2 * s + c
            halo = at_near * near[k : k + 1, :] + at_far * far[k : k + 1, :]
            out[s, c] = partial[s, c] + halo


VMEM = pl.BlockSpec(memory_space=pltpu.VMEM)
SMEM = pl.BlockSpec(memory_space=pltpu.SMEM)
PARAMS = pltpu.CompilerParams(vmem_limit_bytes=24 << 20)


def per_device(object_field, probe_wave, measured, positions, shear_steps, smooth_weight):
    slices = object_field.shape[0]
    tilts, per_owner = measured.shape[:2]
    owners = lax.axis_size("ln")
    tiles = tilts * per_owner
    depth = 2 * slices * ROWS
    table = jnp.asarray(tables())
    tw = jnp.asarray(twiddles())
    rows = slices * OUTER * ROWS
    chunk = (owners, tiles, depth, LANES)
    send = pl.pallas_call(
        shear_kernel,
        out_shape=jax.ShapeDtypeStruct(chunk, BF16),
        in_specs=[SMEM, SMEM, VMEM, VMEM, VMEM],
        out_specs=VMEM,
        scratch_shapes=[
            pltpu.VMEM((rows, 2 * LANES), F32),
            pltpu.VMEM((tilts * rows, 2 * LANES), F32),
            pltpu.VMEM((tilts * rows, 2 * LANES), F32),
            pltpu.VMEM((tilts, depth, COLS + LANES), F32),
        ],
        compiler_params=PARAMS,
        name="shear",
    )(shear_steps, positions, object_field, table[:2], tw)
    recv = lax.all_to_all(send, "ln", 0, 0, tiled=True)
    group = 4
    grads = pl.pallas_call(
        tile_kernel,
        out_shape=jax.ShapeDtypeStruct(chunk, BF16),
        grid=(tiles // group,),
        in_specs=[
            pl.BlockSpec((owners, group, depth, LANES), lambda g: (0, g, 0, 0)),
            pl.BlockSpec((group, LANES, LANES), lambda g: (g, 0, 0)),
            pl.BlockSpec((2, LANES, LANES), lambda g: (0, 0, 0)),
            pl.BlockSpec(table.shape, lambda g: (0, 0, 0, 0)),
        ],
        out_specs=pl.BlockSpec((owners, group, depth, LANES), lambda g: (0, g, 0, 0)),
        compiler_params=PARAMS,
        name="tiles",
    )(recv, measured.reshape(tiles, LANES, LANES), probe_wave, table)
    back = lax.all_to_all(grads, "ln", 0, 0, tiled=True)
    edge = jax.ShapeDtypeStruct((2 * slices, COLS), F32)
    whole = jax.ShapeDtypeStruct((slices, 2, ROWS, COLS), F32)
    partial, near, far = pl.pallas_call(
        descent_kernel,
        out_shape=(whole, edge, edge),
        in_specs=[SMEM, SMEM, VMEM, VMEM, VMEM, VMEM],
        out_specs=(VMEM, VMEM, VMEM),
        scratch_shapes=[pltpu.VMEM((depth, COLS + LANES), F32) for _ in range(2 * tilts)]
        + [pltpu.VMEM((tilts * rows, 2 * LANES), F32), pltpu.VMEM((rows, 2 * LANES), F32)],
        compiler_params=PARAMS,
        name="descent",
    )(shear_steps, positions, back, smooth_weight, table[:2], tw)
    count = lax.axis_size("grp") * owners
    axes = ("grp", "ln")
    between = [(i, i + 1) for i in range(1, count - 1, 2)]
    far = lax.ppermute(far, axes, between + [(j, i) for i, j in between])
    near = lax.ppermute(near, axes, [(i, i ^ 1) for i in range(count)])
    return pl.pallas_call(
        halo_kernel,
        out_shape=whole,
        in_specs=[VMEM] * 4,
        out_specs=VMEM,
        compiler_params=PARAMS,
        name="halo",
    )(partial, near, far, smooth_weight)


def solution(mesh):
    in_specs = (
        P(None, None, ("grp", "ln"), None),
        P(),
        P(None, ("grp", "ln"), None, None),
        P(None, "grp"),
        P(None, ("grp", "ln")),
        P(("grp", "ln"), None),
    )
    out_specs = P(None, None, ("grp", "ln"), None)
    return jax.shard_map(
        per_device, mesh=mesh, in_specs=in_specs, out_specs=out_specs, check_vma=False
    )
```

```python
import functools
import math

import jax
import jax.numpy as jnp
import numpy as np
from jax import lax
from jax.experimental import pallas as pl
from jax.experimental.pallas import tpu as pltpu
from jax.sharding import PartitionSpec as P

AMP_FLOOR = 0.25
FRESNEL = 100.0
SHEAR_UNITS = 8
LANES = 128
OUTER = 16
COLS = OUTER * LANES
ROWS = 8
UNROLL = 4
BF16 = jnp.bfloat16
F32 = jnp.float32


def split_table(table):
    high = np.asarray(table, np.float32).astype(BF16)
    low = (np.asarray(table) - high.astype(np.float64)).astype(np.float32).astype(BF16)
    return np.stack([high, low])


def right_block(matrix):
    top = np.concatenate([matrix.real, matrix.imag], 1)
    bottom = np.concatenate([-matrix.imag, matrix.real], 1)
    return np.concatenate([top, bottom], 0)


def tables():
    counter = np.arange(LANES)
    signed = (counter + LANES // 2) % LANES - LANES // 2
    dft = np.exp(-2j * math.pi / LANES * (counter[:, None] * counter[None, :] % LANES))
    dft = dft / math.sqrt(LANES)
    step = np.exp(-1j * FRESNEL / LANES**2 * signed.astype(np.float64) ** 2)
    spread = (dft.conj() * step[None, :]) @ dft
    fourier = right_block(dft)
    fresnel = right_block(spread)
    return np.stack([split_table(t) for t in (fourier, fourier.T, fresnel, fresnel.T)])


def twiddles():
    turn = np.arange(OUTER)[:, None] * np.arange(LANES)[None, :]
    angle = 2.0 * math.pi / COLS * turn
    return np.stack([np.cos(angle), np.sin(angle)]).astype(np.float32)


def const_mul(value, angle_num, angle_den, sign):
    re, im = value
    eighth = 8 * angle_num / angle_den
    if eighth == 0:
        return value
    if eighth == 2:
        return (-im * sign, re * sign) if sign in (1, -1) else None
    cosine = math.cos(2.0 * math.pi * angle_num / angle_den)
    sine = sign * math.sin(2.0 * math.pi * angle_num / angle_den)
    return (re * cosine - im * sine, re * sine + im * cosine)


def small_dft(values, sign):
    count = len(values)
    if count == 1:
        return values
    even = small_dft(values[::2], sign)
    odd = small_dft(values[1::2], sign)
    out = [None] * count
    for k in range(count // 2):
        re, im = const_mul(odd[k], k, count, sign)
        out[k] = (even[k][0] + re, even[k][1] + im)
        out[k + count // 2] = (even[k][0] - re, even[k][1] - im)
    return out


def cmul(a, b):
    return (a[0] * b[0] - a[1] * b[1], a[0] * b[1] + a[1] * b[0])


def conj_mul(a, b):
    return (a[0] * b[0] + a[1] * b[1], a[0] * b[1] - a[1] * b[0])


def halves(x):
    high = x.astype(BF16)
    return high, (x - high.astype(F32)).astype(BF16)


def dot(a, b):
    return jnp.dot(a, b, preferred_element_type=F32)


def rmul(x, table, which):
    high, low = halves(x)
    top = table[which, 0]
    return dot(high, top) + (dot(low, top) + dot(high, table[which, 1]))


def lmul(table, which, x):
    high, low = halves(x)
    top = table[which, 0]
    return dot(top, high) + (dot(top, low) + dot(table[which, 1], high))


def rmul2(x, table, which):
    high = x.astype(BF16)
    return dot(high, table[which, 0])


def lmul2(table, which, x):
    high = x.astype(BF16)
    return dot(table[which, 0], high)


def shear_factors(shear, tilt):
    row = lax.broadcasted_iota(jnp.int32, (ROWS, LANES), 0)
    lane = lax.broadcasted_iota(jnp.int32, (ROWS, LANES), 1)
    steps = jnp.zeros((ROWS, LANES), jnp.int32)
    for r in range(ROWS):
        steps = jnp.where(row == r, shear[tilt, r], steps)
    units = SHEAR_UNITS * COLS

    def turn(count):
        count = jnp.bitwise_and(count, units - 1)
        count = jnp.where(count >= units // 2, count - units, count)
        angle = (-2.0 * math.pi / units) * count.astype(F32)
        return (jnp.cos(angle), jnp.sin(angle))

    freq = OUTER * lane - jnp.where(lane >= LANES // 2, COLS, 0)
    base = turn(freq * steps)
    first = turn(steps)
    powers = [(jnp.ones((ROWS, LANES), F32), jnp.zeros((ROWS, LANES), F32)), first]
    for i in range(2, OUTER):
        powers.append(cmul(powers[i // 2], powers[i - i // 2]))
    return base, powers


def put(ref, block, value):
    ref[block * ROWS : (block + 1) * ROWS, :LANES] = value[0]
    ref[block * ROWS : (block + 1) * ROWS, LANES:] = value[1]


def get(array, block):
    return (
        array[block * ROWS : (block + 1) * ROWS, :LANES],
        array[block * ROWS : (block + 1) * ROWS, LANES:],
    )


def forward_columns(chunks, tw, ref, base_block):
    mixed = small_dft(chunks, -1)
    for i in range(OUTER):
        w = (tw[0, i : i + 1, :], tw[1, i : i + 1, :])
        put(ref, base_block + i, conj_mul(w, mixed[i]))


def inverse_columns(array, base_block, tw):
    blocks = []
    for i in range(OUTER):
        w = (tw[0, i : i + 1, :] * (1.0 / OUTER), tw[1, i : i + 1, :] * (1.0 / OUTER))
        blocks.append(cmul(w, get(array, base_block + i)))
    return small_dft(blocks, 1)


def shear_kernel(*refs):
    given, out, x_ref, y_ref, z_ref, band = refs[:5], *refs[5:10]
    held, sems = refs[10:15], refs[15]
    copies = [
        pltpu.make_async_copy(src, dst, sems.at[k]) for k, (src, dst) in enumerate(zip(given, held))
    ]
    for copy in copies:
        copy.start()
    obj, tw, table, shear, pos = held
    copies[0].wait()
    copies[1].wait()
    slices = obj.shape[0]
    tilts = band.shape[0]
    for s in range(slices):
        chunks = [
            tuple(obj[s, c, :, j * LANES : (j + 1) * LANES] for c in range(2)) for j in range(OUTER)
        ]
        forward_columns(chunks, tw, x_ref, s * OUTER)
    for copy in copies[2:]:
        copy.wait()
    x_ref[...] = rmul(x_ref[...], table, 0)
    for t in range(tilts):
        base, powers = shear_factors(shear, t)
        for i in range(OUTER):
            phase = cmul(base, powers[i])
            for s in range(slices):
                put(y_ref, (t * slices + s) * OUTER + i, cmul(get(x_ref, s * OUTER + i), phase))
    z_ref[...] = rmul(y_ref[...], table, 1)
    for t in range(tilts):
        for s in range(slices):
            chunks = inverse_columns(z_ref, (t * slices + s) * OUTER, tw)
            for j in range(OUTER):
                for c in range(2):
                    row = (2 * s + c) * ROWS
                    band[t, row : row + ROWS, j * LANES : (j + 1) * LANES] = chunks[j][c]
                    if j == 0:
                        band[t, row : row + ROWS, COLS:] = chunks[j][c]
    depth = band.shape[1]
    lane = lax.broadcasted_iota(jnp.int32, (depth, LANES), 1)
    per_owner = out.shape[1] // tilts

    def some_owners(step, carry):
        for o in range(UNROLL):
            d = step * UNROLL + o
            for jj in range(per_owner):
                for t in range(tilts):
                    p = pos[t, d * per_owner + jj]
                    off = jnp.bitwise_and(p, LANES - 1)
                    start = pl.multiple_of(p - off, LANES)
                    back = jnp.bitwise_and(LANES - off, LANES - 1)
                    near = pltpu.roll(band[t, :, pl.ds(start, LANES)], back, 1)
                    far = pltpu.roll(band[t, :, pl.ds(start + LANES, LANES)], back, 1)
                    window = jnp.where(lane < LANES - off, near, far)
                    out[d, t * per_owner + jj] = window.astype(BF16)
        return carry

    lax.fori_loop(0, out.shape[0] // UNROLL, some_owners, 0)


def both(values, table, right, left):
    tile = LANES
    halved = [rmul2(jnp.concatenate(value, 1), table, right) for value in values]
    stacked = [
        jnp.concatenate(
            [
                jnp.concatenate([half[:tile, :tile], half[tile:, :tile]], 1),
                jnp.concatenate([half[:tile, tile:], half[tile:, tile:]], 1),
            ],
            0,
        )
        for half in halved
    ]
    full = [lmul2(table, left, x) for x in stacked]
    return [
        (
            jnp.concatenate([x[:tile, :tile], x[:tile, tile:]], 0),
            jnp.concatenate([x[tile:, :tile], x[tile:, tile:]], 0),
        )
        for x in full
    ]


def tile_kernel(recv, measured, probe, table, out):
    owners = recv.shape[0]
    pairs = recv.shape[1] // 2
    first, second, target = [], [], []
    for q in range(pairs):
        parts = [[] for _ in range(4)]
        for p in (2 * q, 2 * q + 1):
            for d in range(owners):
                rows = recv[d, p].astype(F32)
                for k in range(4):
                    parts[k].append(rows[k * ROWS : (k + 1) * ROWS])
        parts = [jnp.concatenate(part, 0) for part in parts]
        first.append((parts[0], parts[1]))
        second.append((parts[2], parts[3]))
        target.append(jnp.concatenate([measured[2 * q], measured[2 * q + 1]], 0))
    start = tuple(jnp.concatenate([probe[c]] * 2, 0) for c in range(2))
    wave = both([cmul(start, x) for x in first], table, 2, 3)
    far = both([cmul(w, x) for w, x in zip(wave, second)], table, 0, 1)
    changed = []
    for (re, im), m in zip(far, target):
        factor = 1.0 - m * lax.rsqrt(re * re + im * im + AMP_FLOOR)
        changed.append((factor * re, factor * im))
    back = both(changed, table, 1, 0)
    grad1 = [conj_mul(w, b) for w, b in zip(wave, back)]
    back = both([conj_mul(x, b) for x, b in zip(second, back)], table, 3, 2)
    grad0 = [conj_mul(start, b) for b in back]
    for q in range(pairs):
        grads = (*grad0[q], *grad1[q])
        for p in range(2):
            for d in range(owners):
                row = p * LANES + d * ROWS
                mine = jnp.concatenate([g[row : row + ROWS] for g in grads], 0)
                out[d, 2 * q + p] = mine.astype(BF16)


def descent_kernel(shear, pos, recv, weight, table, tw, out, near, far, *scratch):
    accs, (x_ref, y_ref) = scratch[:-2], scratch[-2:]
    tilts = len(accs) // 2
    per_owner = recv.shape[1] // tilts
    depth = accs[0].shape[0]
    slices = depth // (2 * ROWS)
    for acc in accs:
        acc[...] = jnp.zeros_like(acc)
    lane = lax.broadcasted_iota(jnp.int32, (depth, LANES), 1)

    def some_owners(step, carry):
        for o in range(UNROLL):
            d = step * UNROLL + o
            for jj in range(per_owner):
                for t in range(tilts):
                    acc = accs[t + tilts * (jj % 2)]
                    p = pos[t, d * per_owner + jj]
                    off = jnp.bitwise_and(p, LANES - 1)
                    start = pl.multiple_of(p - off, LANES)
                    moved = pltpu.roll(recv[d, t * per_owner + jj].astype(F32), off, 1)
                    here = lane >= off
                    spread = [jnp.where(here, moved, 0.0), jnp.where(here, 0.0, moved)]
                    acc[:, pl.ds(start, 2 * LANES)] += jnp.concatenate(spread, 1)
        return carry

    lax.fori_loop(0, recv.shape[0] // UNROLL, some_owners, 0)
    for t in range(tilts):
        for s in range(slices):
            chunks = []
            for j in range(OUTER):
                pair = []
                for c in range(2):
                    row = (2 * s + c) * ROWS
                    value = 0.0
                    for acc in (accs[t], accs[t + tilts]):
                        value = value + acc[row : row + ROWS, j * LANES : (j + 1) * LANES]
                        if j == 0:
                            value = value + acc[row : row + ROWS, COLS:]
                    pair.append(value)
                chunks.append(tuple(pair))
            forward_columns(chunks, tw, x_ref, (t * slices + s) * OUTER)
    x_ref[...] = rmul(x_ref[...], table, 0)
    for t in range(tilts):
        base, powers = shear_factors(shear, t)
        for i in range(OUTER):
            phase = cmul(base, powers[i])
            for s in range(slices):
                value = conj_mul(phase, get(x_ref, (t * slices + s) * OUTER + i))
                if t:
                    before = get(y_ref, s * OUTER + i)
                    value = (value[0] + before[0], value[1] + before[1])
                put(y_ref, s * OUTER + i, value)
    y_ref[...] = rmul(y_ref[...], table, 1)
    row = lax.broadcasted_iota(jnp.int32, (ROWS, LANES), 0)
    lane = lax.broadcasted_iota(jnp.int32, (ROWS, LANES), 1)
    odd = lax.rem(lax.axis_index("ln"), 2) == 1
    for s in range(slices):
        chunks = inverse_columns(y_ref, s * OUTER, tw)
        for c in range(2):
            values = [chunk[c] for chunk in chunks]
            ahead = [pltpu.roll(v, 1, 1) for v in values]
            behind = [pltpu.roll(v, LANES - 1, 1) for v in values]
            for j in range(OUTER):
                v = values[j]
                cols = slice(j * LANES, (j + 1) * LANES)
                left = jnp.where(lane == 0, ahead[j - 1], ahead[j])
                right = jnp.where(lane == LANES - 1, behind[(j + 1) % OUTER], behind[j])
                above = jnp.where(row == 0, 0.0, pltpu.roll(v, 1, 0))
                below = jnp.where(row == ROWS - 1, 0.0, pltpu.roll(v, ROWS - 1, 0))
                around = (above + below) + (left + right)
                out[s, c, :, cols] = v + weight[:, cols] * (around - 4.0 * v)
                first, last = v[:1], v[ROWS - 1 :]
                near[2 * s + c : 2 * s + c + 1, cols] = jnp.where(odd, first, last)
                far[2 * s + c : 2 * s + c + 1, cols] = jnp.where(odd, last, first)


def halo_kernel(partial, near, far, weight, out):
    odd = lax.rem(lax.axis_index("ln"), 2) == 1
    row = lax.broadcasted_iota(jnp.int32, weight.shape, 0)
    near_row = jnp.where(odd, 0, ROWS - 1)
    at_near = jnp.where(row == near_row, weight[...], 0.0)
    at_far = jnp.where(row == ROWS - 1 - near_row, weight[...], 0.0)
    for s in range(out.shape[0]):
        for c in range(2):
            k = 2 * s + c
            halo = at_near * near[k : k + 1, :] + at_far * far[k : k + 1, :]
            out[s, c] = partial[s, c] + halo


VMEM = pl.BlockSpec(memory_space=pltpu.VMEM)
SMEM = pl.BlockSpec(memory_space=pltpu.SMEM)
HBM = pl.BlockSpec(memory_space=pltpu.MemorySpace.HBM)
PARAMS = pltpu.CompilerParams(vmem_limit_bytes=24 << 20)


def per_device(object_field, probe_wave, measured, positions, shear_steps, smooth_weight):
    slices = object_field.shape[0]
    tilts, per_owner = measured.shape[:2]
    owners = lax.axis_size("ln")
    tiles = tilts * per_owner
    depth = 2 * slices * ROWS
    table = jnp.asarray(tables())
    tw = jnp.asarray(twiddles())
    fourier = table[:2]
    rows = slices * OUTER * ROWS
    chunk = (owners, tiles, depth, LANES)
    send = pl.pallas_call(
        shear_kernel,
        out_shape=jax.ShapeDtypeStruct(chunk, BF16),
        in_specs=[HBM] * 5,
        out_specs=VMEM,
        scratch_shapes=[
            pltpu.VMEM((rows, 2 * LANES), F32),
            pltpu.VMEM((tilts * rows, 2 * LANES), F32),
            pltpu.VMEM((tilts * rows, 2 * LANES), F32),
            pltpu.VMEM((tilts, depth, COLS + LANES), F32),
            pltpu.VMEM(object_field.shape, F32),
            pltpu.VMEM(tw.shape, F32),
            pltpu.VMEM(fourier.shape, BF16),
            pltpu.SMEM(shear_steps.shape, jnp.int32),
            pltpu.SMEM(positions.shape, jnp.int32),
            pltpu.SemaphoreType.DMA((5,)),
        ],
        compiler_params=PARAMS,
        name="shear",
    )(*[
        pltpu.with_memory_space_constraint(x, pltpu.MemorySpace.HBM)
        for x in (object_field, tw, fourier, shear_steps, positions)
    ])
    recv = lax.all_to_all(send, "ln", 0, 0, tiled=True)
    group = 4
    grads = pl.pallas_call(
        tile_kernel,
        out_shape=jax.ShapeDtypeStruct(chunk, BF16),
        grid=(tiles // group,),
        in_specs=[
            pl.BlockSpec((owners, group, depth, LANES), lambda g: (0, g, 0, 0)),
            pl.BlockSpec((group, LANES, LANES), lambda g: (g, 0, 0)),
            pl.BlockSpec((2, LANES, LANES), lambda g: (0, 0, 0)),
            pl.BlockSpec(table.shape, lambda g: (0, 0, 0, 0)),
        ],
        out_specs=pl.BlockSpec((owners, group, depth, LANES), lambda g: (0, g, 0, 0)),
        compiler_params=PARAMS,
        name="tiles",
    )(recv, measured.reshape(tiles, LANES, LANES), probe_wave, table)
    back = lax.all_to_all(grads, "ln", 0, 0, tiled=True)
    edge = jax.ShapeDtypeStruct((2 * slices, COLS), F32)
    whole = jax.ShapeDtypeStruct((slices, 2, ROWS, COLS), F32)
    partial, near, far = pl.pallas_call(
        descent_kernel,
        out_shape=(whole, edge, edge),
        in_specs=[SMEM, SMEM, VMEM, VMEM, VMEM, VMEM],
        out_specs=(VMEM, VMEM, VMEM),
        scratch_shapes=[pltpu.VMEM((depth, COLS + LANES), F32) for _ in range(2 * tilts)]
        + [pltpu.VMEM((tilts * rows, 2 * LANES), F32), pltpu.VMEM((rows, 2 * LANES), F32)],
        compiler_params=PARAMS,
        name="descent",
    )(shear_steps, positions, back, smooth_weight, fourier, tw)
    count = lax.axis_size("grp") * owners
    axes = ("grp", "ln")
    between = [(i, i + 1) for i in range(1, count - 1, 2)]
    far = lax.ppermute(far, axes, between + [(j, i) for i, j in between])
    near = lax.ppermute(near, axes, [(i, i ^ 1) for i in range(count)])
    return pl.pallas_call(
        halo_kernel,
        out_shape=whole,
        in_specs=[VMEM] * 4,
        out_specs=VMEM,
        compiler_params=PARAMS,
        name="halo",
    )(partial, near, far, smooth_weight)


def solution(mesh):
    in_specs = (
        P(None, None, ("grp", "ln"), None),
        P(),
        P(None, ("grp", "ln"), None, None),
        P(None, "grp"),
        P(None, ("grp", "ln")),
        P(("grp", "ln"), None),
    )
    out_specs = P(None, None, ("grp", "ln"), None)
    return jax.shard_map(
        per_device, mesh=mesh, in_specs=in_specs, out_specs=out_specs, check_vma=False
    )
```

```python
import functools
import math

import jax
import jax.numpy as jnp
import numpy as np
from jax import lax
from jax.experimental import pallas as pl
from jax.experimental.pallas import tpu as pltpu
from jax.sharding import PartitionSpec as P

AMP_FLOOR = 0.25
FRESNEL = 100.0
SHEAR_UNITS = 8
LANES = 128
OUTER = 16
COLS = OUTER * LANES
ROWS = 8
UNROLL = 16
GROUP = 4
BF16 = jnp.bfloat16
F32 = jnp.float32


def split_table(table):
    high = np.asarray(table, np.float32).astype(BF16)
    low = (np.asarray(table) - high.astype(np.float64)).astype(np.float32).astype(BF16)
    return np.stack([high, low])


def right_block(matrix):
    top = np.concatenate([matrix.real, matrix.imag], 1)
    bottom = np.concatenate([-matrix.imag, matrix.real], 1)
    return np.concatenate([top, bottom], 0)


def tables():
    counter = np.arange(LANES)
    signed = (counter + LANES // 2) % LANES - LANES // 2
    dft = np.exp(-2j * math.pi / LANES * (counter[:, None] * counter[None, :] % LANES))
    dft = dft / math.sqrt(LANES)
    step = np.exp(-1j * FRESNEL / LANES**2 * signed.astype(np.float64) ** 2)
    spread = (dft.conj() * step[None, :]) @ dft
    fourier = right_block(dft)
    fresnel = right_block(spread)
    return np.stack([split_table(t) for t in (fourier, fourier.T, fresnel, fresnel.T)])


def twiddles():
    turn = np.arange(OUTER)[:, None] * np.arange(LANES)[None, :]
    angle = 2.0 * math.pi / COLS * turn
    return np.stack([np.cos(angle), np.sin(angle)]).astype(np.float32)


def const_mul(value, angle_num, angle_den, sign):
    re, im = value
    eighth = 8 * angle_num / angle_den
    if eighth == 0:
        return value
    if eighth == 2:
        return (-im * sign, re * sign) if sign in (1, -1) else None
    cosine = math.cos(2.0 * math.pi * angle_num / angle_den)
    sine = sign * math.sin(2.0 * math.pi * angle_num / angle_den)
    return (re * cosine - im * sine, re * sine + im * cosine)


def small_dft(values, sign):
    count = len(values)
    if count == 1:
        return values
    even = small_dft(values[::2], sign)
    odd = small_dft(values[1::2], sign)
    out = [None] * count
    for k in range(count // 2):
        re, im = const_mul(odd[k], k, count, sign)
        out[k] = (even[k][0] + re, even[k][1] + im)
        out[k + count // 2] = (even[k][0] - re, even[k][1] - im)
    return out


def cmul(a, b):
    return (a[0] * b[0] - a[1] * b[1], a[0] * b[1] + a[1] * b[0])


def conj_mul(a, b):
    return (a[0] * b[0] + a[1] * b[1], a[0] * b[1] - a[1] * b[0])


def halves(x):
    high = x.astype(BF16)
    return high, (x - high.astype(F32)).astype(BF16)


def dot(a, b):
    return jnp.dot(a, b, preferred_element_type=F32)


def rmul(x, table, which):
    high, low = halves(x)
    top = table[which, 0]
    return dot(high, top) + (dot(low, top) + dot(high, table[which, 1]))


def lmul(table, which, x):
    high, low = halves(x)
    top = table[which, 0]
    return dot(top, high) + (dot(top, low) + dot(table[which, 1], high))


def rmul2(x, table, which):
    high = x.astype(BF16)
    return dot(high, table[which, 0])


def lmul2(table, which, x):
    high = x.astype(BF16)
    return dot(table[which, 0], high)


def shear_factors(shear, tilt):
    row = lax.broadcasted_iota(jnp.int32, (ROWS, LANES), 0)
    lane = lax.broadcasted_iota(jnp.int32, (ROWS, LANES), 1)
    steps = jnp.zeros((ROWS, LANES), jnp.int32)
    for r in range(ROWS):
        steps = jnp.where(row == r, shear[tilt, r], steps)
    units = SHEAR_UNITS * COLS

    def turn(count):
        count = jnp.bitwise_and(count, units - 1)
        count = jnp.where(count >= units // 2, count - units, count)
        angle = (-2.0 * math.pi / units) * count.astype(F32)
        return (jnp.cos(angle), jnp.sin(angle))

    freq = OUTER * lane - jnp.where(lane >= LANES // 2, COLS, 0)
    base = turn(freq * steps)
    first = turn(steps)
    powers = [(jnp.ones((ROWS, LANES), F32), jnp.zeros((ROWS, LANES), F32)), first]
    for i in range(2, OUTER):
        powers.append(cmul(powers[i // 2], powers[i - i // 2]))
    return base, powers


def put(ref, block, value):
    ref[block * ROWS : (block + 1) * ROWS, :LANES] = value[0]
    ref[block * ROWS : (block + 1) * ROWS, LANES:] = value[1]


def get(array, block):
    return (
        array[block * ROWS : (block + 1) * ROWS, :LANES],
        array[block * ROWS : (block + 1) * ROWS, LANES:],
    )


def forward_columns(chunks, tw, ref, base_block):
    mixed = small_dft(chunks, -1)
    for i in range(OUTER):
        w = (tw[0, i : i + 1, :], tw[1, i : i + 1, :])
        put(ref, base_block + i, conj_mul(w, mixed[i]))


def inverse_columns(array, base_block, tw):
    blocks = []
    for i in range(OUTER):
        w = (tw[0, i : i + 1, :] * (1.0 / OUTER), tw[1, i : i + 1, :] * (1.0 / OUTER))
        blocks.append(cmul(w, get(array, base_block + i)))
    return small_dft(blocks, 1)


def shear_kernel(*refs):
    given, out, x_ref, y_ref, z_ref, band = refs[:5], *refs[5:10]
    held, sems = refs[10:15], refs[15]
    copies = [
        pltpu.make_async_copy(src, dst, sems.at[k]) for k, (src, dst) in enumerate(zip(given, held))
    ]
    for copy in copies:
        copy.start()
    obj, tw, table, shear, pos = held
    copies[0].wait()
    copies[1].wait()
    slices = obj.shape[0]
    tilts = band.shape[0]
    for s in range(slices):
        chunks = [
            tuple(obj[s, c, :, j * LANES : (j + 1) * LANES] for c in range(2)) for j in range(OUTER)
        ]
        forward_columns(chunks, tw, x_ref, s * OUTER)
    for copy in copies[2:]:
        copy.wait()
    x_ref[...] = rmul(x_ref[...], table, 0)
    for t in range(tilts):
        base, powers = shear_factors(shear, t)
        for i in range(OUTER):
            phase = cmul(base, powers[i])
            for s in range(slices):
                put(y_ref, (t * slices + s) * OUTER + i, cmul(get(x_ref, s * OUTER + i), phase))
    z_ref[...] = rmul(y_ref[...], table, 1)
    for t in range(tilts):
        for s in range(slices):
            chunks = inverse_columns(z_ref, (t * slices + s) * OUTER, tw)
            for j in range(OUTER):
                for c in range(2):
                    row = (2 * s + c) * ROWS
                    band[t, row : row + ROWS, j * LANES : (j + 1) * LANES] = chunks[j][c]
                    if j == 0:
                        band[t, row : row + ROWS, COLS:] = chunks[j][c]
    depth = band.shape[1]
    lane = lax.broadcasted_iota(jnp.int32, (depth, LANES), 1)
    per_owner = out.shape[1] // tilts

    def some_owners(step, carry):
        for o in range(UNROLL):
            d = step * UNROLL + o
            for jj in range(per_owner):
                for t in range(tilts):
                    p = pos[t, d * per_owner + jj]
                    off = jnp.bitwise_and(p, LANES - 1)
                    start = pl.multiple_of(p - off, LANES)
                    back = jnp.bitwise_and(LANES - off, LANES - 1)
                    near = pltpu.roll(band[t, :, pl.ds(start, LANES)], back, 1)
                    far = pltpu.roll(band[t, :, pl.ds(start + LANES, LANES)], back, 1)
                    window = jnp.where(lane < LANES - off, near, far)
                    out[d, t * per_owner + jj] = window.astype(BF16)
        return carry

    lax.fori_loop(0, out.shape[0] // UNROLL, some_owners, 0)


def both(values, table, right, left):
    tile = LANES
    halved = [rmul2(jnp.concatenate(value, 1), table, right) for value in values]
    stacked = [
        jnp.concatenate(
            [
                jnp.concatenate([half[:tile, :tile], half[tile:, :tile]], 1),
                jnp.concatenate([half[:tile, tile:], half[tile:, tile:]], 1),
            ],
            0,
        )
        for half in halved
    ]
    full = [lmul2(table, left, x) for x in stacked]
    return [
        (
            jnp.concatenate([x[:tile, :tile], x[:tile, tile:]], 0),
            jnp.concatenate([x[tile:, :tile], x[tile:, tile:]], 0),
        )
        for x in full
    ]


def tile_kernel(recv, measured, probe, table, out):
    pairs = recv.shape[1] // 2
    for q in range(0, pairs, GROUP):
        some_pairs(range(q, min(q + GROUP, pairs)), recv, measured, probe, table, out)


def some_pairs(pairs, recv, measured, probe, table, out):
    owners = recv.shape[0]
    first, second, target = [], [], []
    for q in pairs:
        parts = [[] for _ in range(4)]
        for p in (2 * q, 2 * q + 1):
            for d in range(owners):
                rows = recv[d, p].astype(F32)
                for k in range(4):
                    parts[k].append(rows[k * ROWS : (k + 1) * ROWS])
        parts = [jnp.concatenate(part, 0) for part in parts]
        first.append((parts[0], parts[1]))
        second.append((parts[2], parts[3]))
        target.append(jnp.concatenate([measured[2 * q], measured[2 * q + 1]], 0))
    start = tuple(jnp.concatenate([probe[c]] * 2, 0) for c in range(2))
    wave = both([cmul(start, x) for x in first], table, 2, 3)
    far = both([cmul(w, x) for w, x in zip(wave, second)], table, 0, 1)
    changed = []
    for (re, im), m in zip(far, target):
        factor = 1.0 - m * lax.rsqrt(re * re + im * im + AMP_FLOOR)
        changed.append((factor * re, factor * im))
    back = both(changed, table, 1, 0)
    grad1 = [conj_mul(w, b) for w, b in zip(wave, back)]
    back = both([conj_mul(x, b) for x, b in zip(second, back)], table, 3, 2)
    grad0 = [conj_mul(start, b) for b in back]
    for k, q in enumerate(pairs):
        grads = (*grad0[k], *grad1[k])
        for p in range(2):
            for d in range(owners):
                row = p * LANES + d * ROWS
                mine = jnp.concatenate([g[row : row + ROWS] for g in grads], 0)
                out[d, 2 * q + p] = mine.astype(BF16)


def descent_kernel(shear, pos, recv, weight, table, tw, out, near, far, *scratch):
    accs, (x_ref, y_ref) = scratch[:-2], scratch[-2:]
    tilts = len(accs) // 2
    per_owner = recv.shape[1] // tilts
    depth = accs[0].shape[0]
    slices = depth // (2 * ROWS)
    for acc in accs:
        acc[...] = jnp.zeros_like(acc)
    lane = lax.broadcasted_iota(jnp.int32, (depth, LANES), 1)

    def some_owners(step, carry):
        for o in range(UNROLL):
            d = step * UNROLL + o
            for jj in range(per_owner):
                for t in range(tilts):
                    acc = accs[t + tilts * (jj % 2)]
                    p = pos[t, d * per_owner + jj]
                    off = jnp.bitwise_and(p, LANES - 1)
                    start = pl.multiple_of(p - off, LANES)
                    moved = pltpu.roll(recv[d, t * per_owner + jj].astype(F32), off, 1)
                    here = lane >= off
                    spread = [jnp.where(here, moved, 0.0), jnp.where(here, 0.0, moved)]
                    acc[:, pl.ds(start, 2 * LANES)] += jnp.concatenate(spread, 1)
        return carry

    lax.fori_loop(0, recv.shape[0] // UNROLL, some_owners, 0)
    for t in range(tilts):
        for s in range(slices):
            chunks = []
            for j in range(OUTER):
                pair = []
                for c in range(2):
                    row = (2 * s + c) * ROWS
                    value = 0.0
                    for acc in (accs[t], accs[t + tilts]):
                        value = value + acc[row : row + ROWS, j * LANES : (j + 1) * LANES]
                        if j == 0:
                            value = value + acc[row : row + ROWS, COLS:]
                    pair.append(value)
                chunks.append(tuple(pair))
            forward_columns(chunks, tw, x_ref, (t * slices + s) * OUTER)
    x_ref[...] = rmul(x_ref[...], table, 0)
    for t in range(tilts):
        base, powers = shear_factors(shear, t)
        for i in range(OUTER):
            phase = cmul(base, powers[i])
            for s in range(slices):
                value = conj_mul(phase, get(x_ref, (t * slices + s) * OUTER + i))
                if t:
                    before = get(y_ref, s * OUTER + i)
                    value = (value[0] + before[0], value[1] + before[1])
                put(y_ref, s * OUTER + i, value)
    y_ref[...] = rmul(y_ref[...], table, 1)
    row = lax.broadcasted_iota(jnp.int32, (ROWS, LANES), 0)
    lane = lax.broadcasted_iota(jnp.int32, (ROWS, LANES), 1)
    odd = lax.rem(lax.axis_index("ln"), 2) == 1
    for s in range(slices):
        chunks = inverse_columns(y_ref, s * OUTER, tw)
        for c in range(2):
            values = [chunk[c] for chunk in chunks]
            ahead = [pltpu.roll(v, 1, 1) for v in values]
            behind = [pltpu.roll(v, LANES - 1, 1) for v in values]
            for j in range(OUTER):
                v = values[j]
                cols = slice(j * LANES, (j + 1) * LANES)
                left = jnp.where(lane == 0, ahead[j - 1], ahead[j])
                right = jnp.where(lane == LANES - 1, behind[(j + 1) % OUTER], behind[j])
                above = jnp.where(row == 0, 0.0, pltpu.roll(v, 1, 0))
                below = jnp.where(row == ROWS - 1, 0.0, pltpu.roll(v, ROWS - 1, 0))
                around = (above + below) + (left + right)
                out[s, c, :, cols] = v + weight[:, cols] * (around - 4.0 * v)
                first, last = v[:1], v[ROWS - 1 :]
                near[2 * s + c : 2 * s + c + 1, cols] = jnp.where(odd, first, last)
                far[2 * s + c : 2 * s + c + 1, cols] = jnp.where(odd, last, first)


def halo_kernel(partial, far, near, weight, out):
    odd = lax.rem(lax.axis_index("ln"), 2) == 1
    row = lax.broadcasted_iota(jnp.int32, weight.shape, 0)
    near_row = jnp.where(odd, 0, ROWS - 1)
    at_near = jnp.where(row == near_row, weight[...], 0.0)
    at_far = jnp.where(row == ROWS - 1 - near_row, weight[...], 0.0)
    for s in range(out.shape[0]):
        for c in range(2):
            k = 2 * s + c
            halo = at_near * near[k : k + 1, :] + at_far * far[k : k + 1, :]
            out[s, c] = partial[s, c] + halo


VMEM = pl.BlockSpec(memory_space=pltpu.VMEM)
SMEM = pl.BlockSpec(memory_space=pltpu.SMEM)
HBM = pl.BlockSpec(memory_space=pltpu.MemorySpace.HBM)
PARAMS = pltpu.CompilerParams(vmem_limit_bytes=24 << 20)


def per_device(object_field, probe_wave, measured, positions, shear_steps, smooth_weight):
    slices = object_field.shape[0]
    tilts, per_owner = measured.shape[:2]
    owners = lax.axis_size("ln")
    tiles = tilts * per_owner
    depth = 2 * slices * ROWS
    table = jnp.asarray(tables())
    tw = jnp.asarray(twiddles())
    fourier = table[:2]
    rows = slices * OUTER * ROWS
    chunk = (owners, tiles, depth, LANES)
    send = pl.pallas_call(
        shear_kernel,
        out_shape=jax.ShapeDtypeStruct(chunk, BF16),
        in_specs=[HBM] * 5,
        out_specs=VMEM,
        scratch_shapes=[
            pltpu.VMEM((rows, 2 * LANES), F32),
            pltpu.VMEM((tilts * rows, 2 * LANES), F32),
            pltpu.VMEM((tilts * rows, 2 * LANES), F32),
            pltpu.VMEM((tilts, depth, COLS + LANES), F32),
            pltpu.VMEM(object_field.shape, F32),
            pltpu.VMEM(tw.shape, F32),
            pltpu.VMEM(fourier.shape, BF16),
            pltpu.SMEM(shear_steps.shape, jnp.int32),
            pltpu.SMEM(positions.shape, jnp.int32),
            pltpu.SemaphoreType.DMA((5,)),
        ],
        compiler_params=PARAMS,
        name="shear",
    )(*[
        pltpu.with_memory_space_constraint(x, pltpu.MemorySpace.HBM)
        for x in (object_field, tw, fourier, shear_steps, positions)
    ])
    recv = lax.all_to_all(send, "ln", 0, 0, tiled=True)
    grads = pl.pallas_call(
        tile_kernel,
        out_shape=jax.ShapeDtypeStruct(chunk, BF16),
        in_specs=[VMEM] * 4,
        out_specs=VMEM,
        compiler_params=PARAMS,
        name="tiles",
    )(recv, measured.reshape(tiles, LANES, LANES), probe_wave, table)
    back = lax.all_to_all(grads, "ln", 0, 0, tiled=True)
    edge = jax.ShapeDtypeStruct((2 * slices, COLS), F32)
    whole = jax.ShapeDtypeStruct((slices, 2, ROWS, COLS), F32)
    partial, near, far = pl.pallas_call(
        descent_kernel,
        out_shape=(whole, edge, edge),
        in_specs=[SMEM, SMEM, VMEM, VMEM, VMEM, VMEM],
        out_specs=(VMEM, VMEM, VMEM),
        scratch_shapes=[pltpu.VMEM((depth, COLS + LANES), F32) for _ in range(2 * tilts)]
        + [pltpu.VMEM((tilts * rows, 2 * LANES), F32), pltpu.VMEM((rows, 2 * LANES), F32)],
        compiler_params=PARAMS,
        name="descent",
    )(shear_steps, positions, back, smooth_weight, fourier, tw)
    count = lax.axis_size("grp") * owners
    axes = ("grp", "ln")
    between = [(i, i + 1) for i in range(1, count - 1, 2)]
    near = lax.ppermute(near, axes, [(i, i ^ 1) for i in range(count)])
    far = lax.ppermute(far, axes, between + [(j, i) for i, j in between])
    return pl.pallas_call(
        halo_kernel,
        out_shape=whole,
        in_specs=[VMEM] * 4,
        out_specs=VMEM,
        compiler_params=PARAMS,
        name="halo",
    )(partial, far, near, smooth_weight)


def solution(mesh):
    in_specs = (
        P(None, None, ("grp", "ln"), None),
        P(),
        P(None, ("grp", "ln"), None, None),
        P(None, "grp"),
        P(None, ("grp", "ln")),
        P(("grp", "ln"), None),
    )
    out_specs = P(None, None, ("grp", "ln"), None)
    return jax.shard_map(
        per_device, mesh=mesh, in_specs=in_specs, out_specs=out_specs, check_vma=False
    )
```

```python
import functools
import math

import jax
import jax.numpy as jnp
import numpy as np
from jax import lax
from jax.experimental import pallas as pl
from jax.experimental.pallas import tpu as pltpu
from jax.sharding import PartitionSpec as P

AMP_FLOOR = 0.25
FRESNEL = 100.0
SHEAR_UNITS = 8
LANES = 128
OUTER = 16
COLS = OUTER * LANES
ROWS = 8
UNROLL = 16
GROUP = 4
BF16 = jnp.bfloat16
F32 = jnp.float32


def split_table(table):
    high = np.asarray(table, np.float32).astype(BF16)
    low = (np.asarray(table) - high.astype(np.float64)).astype(np.float32).astype(BF16)
    return np.stack([high, low])


def right_block(matrix):
    top = np.concatenate([matrix.real, matrix.imag], 1)
    bottom = np.concatenate([-matrix.imag, matrix.real], 1)
    return np.concatenate([top, bottom], 0)


def tables():
    counter = np.arange(LANES)
    signed = (counter + LANES // 2) % LANES - LANES // 2
    dft = np.exp(-2j * math.pi / LANES * (counter[:, None] * counter[None, :] % LANES))
    dft = dft / math.sqrt(LANES)
    step = np.exp(-1j * FRESNEL / LANES**2 * signed.astype(np.float64) ** 2)
    spread = (dft.conj() * step[None, :]) @ dft
    fourier = right_block(dft)
    fresnel = right_block(spread)
    return np.stack([split_table(t) for t in (fourier, fourier.T, fresnel, fresnel.T)])


def twiddles():
    turn = np.arange(OUTER)[:, None] * np.arange(LANES)[None, :]
    angle = 2.0 * math.pi / COLS * turn
    return np.stack([np.cos(angle), np.sin(angle)]).astype(np.float32)


def const_mul(value, angle_num, angle_den, sign):
    re, im = value
    eighth = 8 * angle_num / angle_den
    if eighth == 0:
        return value
    if eighth == 2:
        return (-im * sign, re * sign) if sign in (1, -1) else None
    cosine = math.cos(2.0 * math.pi * angle_num / angle_den)
    sine = sign * math.sin(2.0 * math.pi * angle_num / angle_den)
    return (re * cosine - im * sine, re * sine + im * cosine)


def small_dft(values, sign):
    count = len(values)
    if count == 1:
        return values
    even = small_dft(values[::2], sign)
    odd = small_dft(values[1::2], sign)
    out = [None] * count
    for k in range(count // 2):
        re, im = const_mul(odd[k], k, count, sign)
        out[k] = (even[k][0] + re, even[k][1] + im)
        out[k + count // 2] = (even[k][0] - re, even[k][1] - im)
    return out


def cmul(a, b):
    return (a[0] * b[0] - a[1] * b[1], a[0] * b[1] + a[1] * b[0])


def conj_mul(a, b):
    return (a[0] * b[0] + a[1] * b[1], a[0] * b[1] - a[1] * b[0])


def halves(x):
    high = x.astype(BF16)
    return high, (x - high.astype(F32)).astype(BF16)


def dot(a, b):
    return jnp.dot(a, b, preferred_element_type=F32)


def rmul(x, table, which):
    high, low = halves(x)
    top = table[which, 0]
    return dot(high, top) + (dot(low, top) + dot(high, table[which, 1]))


def lmul(table, which, x):
    high, low = halves(x)
    top = table[which, 0]
    return dot(top, high) + (dot(top, low) + dot(table[which, 1], high))


def rmul2(x, table, which):
    high = x.astype(BF16)
    return dot(high, table[which, 0])


def lmul2(table, which, x):
    high = x.astype(BF16)
    return dot(table[which, 0], high)


def shear_factors(shear, tilt):
    row = lax.broadcasted_iota(jnp.int32, (ROWS, LANES), 0)
    lane = lax.broadcasted_iota(jnp.int32, (ROWS, LANES), 1)
    steps = jnp.zeros((ROWS, LANES), jnp.int32)
    for r in range(ROWS):
        steps = jnp.where(row == r, shear[tilt, r], steps)
    units = SHEAR_UNITS * COLS

    def turn(count):
        count = jnp.bitwise_and(count, units - 1)
        count = jnp.where(count >= units // 2, count - units, count)
        angle = (-2.0 * math.pi / units) * count.astype(F32)
        return (jnp.cos(angle), jnp.sin(angle))

    freq = OUTER * lane - jnp.where(lane >= LANES // 2, COLS, 0)
    base = turn(freq * steps)
    first = turn(steps)
    powers = [(jnp.ones((ROWS, LANES), F32), jnp.zeros((ROWS, LANES), F32)), first]
    for i in range(2, OUTER):
        powers.append(cmul(powers[i // 2], powers[i - i // 2]))
    return base, powers


def put(ref, block, value):
    ref[block * ROWS : (block + 1) * ROWS, :LANES] = value[0]
    ref[block * ROWS : (block + 1) * ROWS, LANES:] = value[1]


def get(array, block):
    return (
        array[block * ROWS : (block + 1) * ROWS, :LANES],
        array[block * ROWS : (block + 1) * ROWS, LANES:],
    )


def forward_columns(chunks, tw, ref, base_block):
    mixed = small_dft(chunks, -1)
    for i in range(OUTER):
        w = (tw[0, i : i + 1, :], tw[1, i : i + 1, :])
        put(ref, base_block + i, conj_mul(w, mixed[i]))


def inverse_columns(array, base_block, tw):
    blocks = []
    for i in range(OUTER):
        w = (tw[0, i : i + 1, :] * (1.0 / OUTER), tw[1, i : i + 1, :] * (1.0 / OUTER))
        blocks.append(cmul(w, get(array, base_block + i)))
    return small_dft(blocks, 1)


def shear_kernel(*refs):
    given, out, x_ref, y_ref, z_ref, band = refs[:5], *refs[5:10]
    held, sems = refs[10:15], refs[15]
    copies = [
        pltpu.make_async_copy(src, dst, sems.at[k]) for k, (src, dst) in enumerate(zip(given, held))
    ]
    for copy in copies:
        copy.start()
    obj, tw, table, shear, pos = held
    copies[0].wait()
    copies[1].wait()
    slices = obj.shape[0]
    tilts = band.shape[0]
    for s in range(slices):
        chunks = [
            tuple(obj[s, c, :, j * LANES : (j + 1) * LANES] for c in range(2)) for j in range(OUTER)
        ]
        forward_columns(chunks, tw, x_ref, s * OUTER)
    for copy in copies[2:]:
        copy.wait()
    x_ref[...] = rmul(x_ref[...], table, 0)
    for t in range(tilts):
        base, powers = shear_factors(shear, t)
        for i in range(OUTER):
            phase = cmul(base, powers[i])
            for s in range(slices):
                put(y_ref, (t * slices + s) * OUTER + i, cmul(get(x_ref, s * OUTER + i), phase))
    z_ref[...] = rmul(y_ref[...], table, 1)
    for t in range(tilts):
        for s in range(slices):
            chunks = inverse_columns(z_ref, (t * slices + s) * OUTER, tw)
            for j in range(OUTER):
                for c in range(2):
                    row = (2 * s + c) * ROWS
                    band[t, row : row + ROWS, j * LANES : (j + 1) * LANES] = chunks[j][c]
                    if j == 0:
                        band[t, row : row + ROWS, COLS:] = chunks[j][c]
    depth = band.shape[1]
    lane = lax.broadcasted_iota(jnp.int32, (depth, LANES), 1)
    per_owner = out.shape[1] // tilts

    def some_owners(step, carry):
        for o in range(UNROLL):
            d = step * UNROLL + o
            for jj in range(per_owner):
                for t in range(tilts):
                    p = pos[t, d * per_owner + jj]
                    off = jnp.bitwise_and(p, LANES - 1)
                    start = pl.multiple_of(p - off, LANES)
                    back = jnp.bitwise_and(LANES - off, LANES - 1)
                    near = pltpu.roll(band[t, :, pl.ds(start, LANES)], back, 1)
                    far = pltpu.roll(band[t, :, pl.ds(start + LANES, LANES)], back, 1)
                    window = jnp.where(lane < LANES - off, near, far)
                    out[d, t * per_owner + jj] = window.astype(BF16)
        return carry

    lax.fori_loop(0, out.shape[0] // UNROLL, some_owners, 0)


def both(values, table, right, left):
    tile = LANES
    rows = 2 * tile
    flat = jnp.concatenate([jnp.concatenate(value, 1) for value in values], 0)
    flat = rmul2(flat, table, right)
    halved = [flat[k * rows : (k + 1) * rows] for k in range(len(values))]
    stacked = [
        jnp.concatenate(
            [
                jnp.concatenate([half[:tile, :tile], half[tile:, :tile]], 1),
                jnp.concatenate([half[:tile, tile:], half[tile:, tile:]], 1),
            ],
            0,
        )
        for half in halved
    ]
    full = [lmul2(table, left, x) for x in stacked]
    return [
        (
            jnp.concatenate([x[:tile, :tile], x[:tile, tile:]], 0),
            jnp.concatenate([x[tile:, :tile], x[tile:, tile:]], 0),
        )
        for x in full
    ]


def tile_kernel(recv, measured, probe, table, out):
    pairs = recv.shape[1] // 2
    for q in range(0, pairs, GROUP):
        some_pairs(range(q, min(q + GROUP, pairs)), recv, measured, probe, table, out)


def some_pairs(pairs, recv, measured, probe, table, out):
    owners = recv.shape[0]
    first, second, target = [], [], []
    for q in pairs:
        parts = [[] for _ in range(4)]
        for p in (2 * q, 2 * q + 1):
            for d in range(owners):
                rows = recv[d, p].astype(F32)
                for k in range(4):
                    parts[k].append(rows[k * ROWS : (k + 1) * ROWS])
        parts = [jnp.concatenate(part, 0) for part in parts]
        first.append((parts[0], parts[1]))
        second.append((parts[2], parts[3]))
        target.append(jnp.concatenate([measured[2 * q], measured[2 * q + 1]], 0))
    start = tuple(jnp.concatenate([probe[c]] * 2, 0) for c in range(2))
    wave = both([cmul(start, x) for x in first], table, 2, 3)
    far = both([cmul(w, x) for w, x in zip(wave, second)], table, 0, 1)
    changed = []
    for (re, im), m in zip(far, target):
        factor = 1.0 - m * lax.rsqrt(re * re + im * im + AMP_FLOOR)
        changed.append((factor * re, factor * im))
    back = both(changed, table, 1, 0)
    grad1 = [conj_mul(w, b) for w, b in zip(wave, back)]
    back = both([conj_mul(x, b) for x, b in zip(second, back)], table, 3, 2)
    grad0 = [conj_mul(start, b) for b in back]
    for k, q in enumerate(pairs):
        grads = (*grad0[k], *grad1[k])
        for p in range(2):
            for d in range(owners):
                row = p * LANES + d * ROWS
                mine = jnp.concatenate([g[row : row + ROWS] for g in grads], 0)
                out[d, 2 * q + p] = mine.astype(BF16)


def descent_kernel(shear, pos, recv, table, tw, out, near, far, *scratch):
    accs, (x_ref, y_ref) = scratch[:-2], scratch[-2:]
    tilts = len(accs) // 2
    per_owner = recv.shape[1] // tilts
    depth = accs[0].shape[0]
    slices = depth // (2 * ROWS)
    for acc in accs:
        acc[...] = jnp.zeros_like(acc)
    lane = lax.broadcasted_iota(jnp.int32, (depth, LANES), 1)

    def some_owners(step, carry):
        for o in range(UNROLL):
            d = step * UNROLL + o
            for jj in range(per_owner):
                for t in range(tilts):
                    acc = accs[t + tilts * (jj % 2)]
                    p = pos[t, d * per_owner + jj]
                    off = jnp.bitwise_and(p, LANES - 1)
                    start = pl.multiple_of(p - off, LANES)
                    moved = pltpu.roll(recv[d, t * per_owner + jj].astype(F32), off, 1)
                    here = lane >= off
                    spread = [jnp.where(here, moved, 0.0), jnp.where(here, 0.0, moved)]
                    acc[:, pl.ds(start, 2 * LANES)] += jnp.concatenate(spread, 1)
        return carry

    lax.fori_loop(0, recv.shape[0] // UNROLL, some_owners, 0)
    for t in range(tilts):
        for s in range(slices):
            chunks = []
            for j in range(OUTER):
                pair = []
                for c in range(2):
                    row = (2 * s + c) * ROWS
                    value = 0.0
                    for acc in (accs[t], accs[t + tilts]):
                        value = value + acc[row : row + ROWS, j * LANES : (j + 1) * LANES]
                        if j == 0:
                            value = value + acc[row : row + ROWS, COLS:]
                    pair.append(value)
                chunks.append(tuple(pair))
            forward_columns(chunks, tw, x_ref, (t * slices + s) * OUTER)
    x_ref[...] = rmul(x_ref[...], table, 0)
    for t in range(tilts):
        base, powers = shear_factors(shear, t)
        for i in range(OUTER):
            phase = cmul(base, powers[i])
            for s in range(slices):
                value = conj_mul(phase, get(x_ref, (t * slices + s) * OUTER + i))
                if t:
                    before = get(y_ref, s * OUTER + i)
                    value = (value[0] + before[0], value[1] + before[1])
                put(y_ref, s * OUTER + i, value)
    y_ref[...] = rmul(y_ref[...], table, 1)
    odd = lax.rem(lax.axis_index("ln"), 2) == 1
    for s in range(slices):
        chunks = inverse_columns(y_ref, s * OUTER, tw)
        for c in range(2):
            k = 2 * s + c
            for j in range(OUTER):
                v = chunks[j][c]
                cols = slice(j * LANES, (j + 1) * LANES)
                out[s, c, :, cols] = v
                first, last = v[:1], v[ROWS - 1 :]
                near[k : k + 1, cols] = jnp.where(odd, first, last)
                far[k : k + 1, cols] = jnp.where(odd, last, first)


def smooth_kernel(descent, weight, out):
    row = lax.broadcasted_iota(jnp.int32, (ROWS, LANES), 0)
    lane = lax.broadcasted_iota(jnp.int32, (ROWS, LANES), 1)
    for s in range(out.shape[0]):
        for c in range(2):
            values = [descent[s, c, :, j * LANES : (j + 1) * LANES] for j in range(OUTER)]
            ahead = [pltpu.roll(v, 1, 1) for v in values]
            behind = [pltpu.roll(v, LANES - 1, 1) for v in values]
            for j in range(OUTER):
                v = values[j]
                cols = slice(j * LANES, (j + 1) * LANES)
                left = jnp.where(lane == 0, ahead[j - 1], ahead[j])
                right = jnp.where(lane == LANES - 1, behind[(j + 1) % OUTER], behind[j])
                above = jnp.where(row == 0, 0.0, pltpu.roll(v, 1, 0))
                below = jnp.where(row == ROWS - 1, 0.0, pltpu.roll(v, ROWS - 1, 0))
                around = (above + below) + (left + right)
                out[s, c, :, cols] = v + weight[:, cols] * (around - 4.0 * v)


def halo_kernel(partial, far, near, weight, out):
    odd = lax.rem(lax.axis_index("ln"), 2) == 1
    row = lax.broadcasted_iota(jnp.int32, weight.shape, 0)
    near_row = jnp.where(odd, 0, ROWS - 1)
    at_near = jnp.where(row == near_row, weight[...], 0.0)
    at_far = jnp.where(row == ROWS - 1 - near_row, weight[...], 0.0)
    for s in range(out.shape[0]):
        for c in range(2):
            k = 2 * s + c
            halo = at_near * near[k : k + 1, :] + at_far * far[k : k + 1, :]
            out[s, c] = partial[s, c] + halo


VMEM = pl.BlockSpec(memory_space=pltpu.VMEM)
SMEM = pl.BlockSpec(memory_space=pltpu.SMEM)
HBM = pl.BlockSpec(memory_space=pltpu.MemorySpace.HBM)
PARAMS = pltpu.CompilerParams(vmem_limit_bytes=24 << 20)


def per_device(object_field, probe_wave, measured, positions, shear_steps, smooth_weight):
    slices = object_field.shape[0]
    tilts, per_owner = measured.shape[:2]
    owners = lax.axis_size("ln")
    tiles = tilts * per_owner
    depth = 2 * slices * ROWS
    table = jnp.asarray(tables())
    tw = jnp.asarray(twiddles())
    fourier = table[:2]
    rows = slices * OUTER * ROWS
    chunk = (owners, tiles, depth, LANES)
    send = pl.pallas_call(
        shear_kernel,
        out_shape=jax.ShapeDtypeStruct(chunk, BF16),
        in_specs=[HBM] * 5,
        out_specs=VMEM,
        scratch_shapes=[
            pltpu.VMEM((rows, 2 * LANES), F32),
            pltpu.VMEM((tilts * rows, 2 * LANES), F32),
            pltpu.VMEM((tilts * rows, 2 * LANES), F32),
            pltpu.VMEM((tilts, depth, COLS + LANES), F32),
            pltpu.VMEM(object_field.shape, F32),
            pltpu.VMEM(tw.shape, F32),
            pltpu.VMEM(fourier.shape, BF16),
            pltpu.SMEM(shear_steps.shape, jnp.int32),
            pltpu.SMEM(positions.shape, jnp.int32),
            pltpu.SemaphoreType.DMA((5,)),
        ],
        compiler_params=PARAMS,
        name="shear",
    )(*[
        pltpu.with_memory_space_constraint(x, pltpu.MemorySpace.HBM)
        for x in (object_field, tw, fourier, shear_steps, positions)
    ])
    recv = lax.all_to_all(send, "ln", 0, 0, tiled=True)
    grads = pl.pallas_call(
        tile_kernel,
        out_shape=jax.ShapeDtypeStruct(chunk, BF16),
        in_specs=[VMEM] * 4,
        out_specs=VMEM,
        compiler_params=PARAMS,
        name="tiles",
    )(recv, measured.reshape(tiles, LANES, LANES), probe_wave, table)
    back = lax.all_to_all(grads, "ln", 0, 0, tiled=True)
    edge = jax.ShapeDtypeStruct((2 * slices, COLS), F32)
    whole = jax.ShapeDtypeStruct((slices, 2, ROWS, COLS), F32)
    descent, near, far = pl.pallas_call(
        descent_kernel,
        out_shape=(whole, edge, edge),
        in_specs=[SMEM, SMEM, VMEM, VMEM, VMEM],
        out_specs=(VMEM, VMEM, VMEM),
        scratch_shapes=[pltpu.VMEM((depth, COLS + LANES), F32) for _ in range(2 * tilts)]
        + [pltpu.VMEM((tilts * rows, 2 * LANES), F32), pltpu.VMEM((rows, 2 * LANES), F32)],
        compiler_params=PARAMS,
        name="descent",
    )(shear_steps, positions, back, fourier, tw)
    count = lax.axis_size("grp") * owners
    axes = ("grp", "ln")
    between = [(i, i + 1) for i in range(1, count - 1, 2)]
    near = lax.ppermute(near, axes, [(i, i ^ 1) for i in range(count)])
    far = lax.ppermute(far, axes, between + [(j, i) for i, j in between])
    partial = pl.pallas_call(
        smooth_kernel,
        out_shape=whole,
        in_specs=[VMEM] * 2,
        out_specs=VMEM,
        compiler_params=PARAMS,
        cost_estimate=pl.CostEstimate(flops=1 << 22, bytes_accessed=1 << 20, transcendentals=0),
        name="smooth",
    )(descent, smooth_weight)
    return pl.pallas_call(
        halo_kernel,
        out_shape=whole,
        in_specs=[VMEM] * 4,
        out_specs=VMEM,
        compiler_params=PARAMS,
        name="halo",
    )(partial, far, near, smooth_weight)


def solution(mesh):
    in_specs = (
        P(None, None, ("grp", "ln"), None),
        P(),
        P(None, ("grp", "ln"), None, None),
        P(None, "grp"),
        P(None, ("grp", "ln")),
        P(("grp", "ln"), None),
    )
    out_specs = P(None, None, ("grp", "ln"), None)
    return jax.shard_map(
        per_device, mesh=mesh, in_specs=in_specs, out_specs=out_specs, check_vma=False
    )
```
